128 devices in a mesh: user: 8 (over y_hi, z), cand: 16 (over x, y_lo, core).
Axes of the slice: x: 4, y: 4 (y_hi: 2, y_lo: 2; y = y_hi * 2 + y_lo), z: 4, core: 2. Of those that a mesh axis runs over, the one named last changes fastest.
Arguments:
- cand_x: bfloat16 [65536, 1024], P(('user', 'cand')), may hold values from -6 to 6
- cand_user: int32 [65536, 1], P(('user', 'cand')), may hold values from 0 to 15; in each aligned block of 512 rows (0 to 511, 512 to 1023, ...) at most 64 rows name the same one
- visible: int32 [65536], P(('user', 'cand')), may hold values from 1 to 16
- hist_len: int32 [16], P('cand'), may hold values from 1 to 2048
- kv_cache: bfloat16 [16, 2048, 2048], P('cand', 'user'), may hold values from -6 to 6
- w_in: bfloat16 [1024, 2048], replicated, may hold values from -0.1875 to 0.1875
- w_out: bfloat16 [1024, 1024], replicated, may hold values from -0.1875 to 0.1875
- ln_gain: float32 [1024], replicated, may hold values from 0.1 to 1.9
Outputs:
- scored: bfloat16 [65536, 1024], P(('user', 'cand'))
The draws below stay inside these ranges and needn't reach their ends.
Inputs may be any that keep to these rules, and one draw needn't show every extreme that they name: `cand_user`: among the 512 candidates of one device no user is named more than 64 times, a bound that some block reaches.
All inputs are finite; a program needn't handle non-finite values.
Results may differ from the reference program's by a relative error of at most 0.0055.
Values may be sent and summed in bfloat16 or wider, within the bound.
A program may use at most 128 MiB of HBM per device.

```python
import math
import jax
import jax.numpy as jnp
import numpy as np
from jax import lax

D = 1024
HEADS = 8
BLK = 128
CAND_DEV = 512
HIST = 2048
HB = 16
USERS = 16
CANDS = 65536
CAP = 64


def place_ends(array, key, least, largest):
    place = [jax.random.randint(jax.random.fold_in(key, axis), (), 0, length) for axis, length in enumerate(array.shape)]
    longest = array.shape.index(max(array.shape))
    next_to = place[:longest] + [(place[longest] + 1) % array.shape[longest]] + place[longest + 1:]
    return array.at[tuple(place)].set(least).at[tuple(next_to)].set(largest)


def levels(rng, extent, cuts, least, largest):
    def one(dim, shards_of):
        draws = jax.random.uniform(jax.random.fold_in(jax.random.fold_in(rng, 6), dim), (shards_of,), jnp.float32, least / len(cuts), largest / len(cuts))
        return jnp.repeat(jnp.exp(draws), extent[dim] // shards_of).reshape((-1,) + (1,) * (len(extent) - dim - 1))

    factor_of = one(*cuts[0])
    for cut in cuts[1:]:
        factor_of = factor_of * one(*cut)
    return factor_of


def deal_out(own_key, own, number, rows, count, top, reach, slope):
    order = jax.random.permutation(own_key, count)
    crowded, ordinary = shares(count, rows * top, reach, slope, True), shares(count, rows * top, reach, slope, False)
    places = jnp.arange(count)

    def named(lengths, turn):
        used = int((lengths > 0).sum())
        fixed = max(1, used // 4)
        shifted = fixed + (places - fixed + turn * (used - fixed)) % max(1, count - fixed)
        return jnp.zeros((count,), jnp.int32).at[order[jnp.where(places < fixed, places, shifted)]].set(jnp.asarray(lengths, jnp.int32))

    lengths = jnp.where(number % 4 == 0, named(crowded, number // 4), named(ordinary, number - number // 4 - 1))
    mixed = jax.random.permutation(jax.random.fold_in(own, 3), count)
    source_of, sink = mixed[0:count // 2 * 2:2], mixed[1:count // 2 * 2:2]
    slack = jnp.minimum(lengths[source_of] - 1, reach - lengths[sink]) // 2
    slack = jnp.where((source_of == order[0]) | (sink == order[0]) | (lengths[sink] == 0), 0, jnp.maximum(slack, 0))
    shifted = jax.random.randint(jax.random.fold_in(own, 4), (count // 2,), 0, 1 << 20) % (slack + 1)
    lengths = lengths.at[source_of].add(-shifted).at[sink].add(shifted)
    items = jnp.searchsorted(jnp.cumsum(lengths), jnp.arange(rows * top), side="right").astype(jnp.int32)
    table = items.reshape(top, rows).T
    table = table[jax.random.permutation(jax.random.fold_in(own, 1), rows)]
    turn = jax.random.randint(jax.random.fold_in(own, 2), (rows, 1), 0, top)
    return jnp.take_along_axis(table, (jnp.arange(top)[None, :] + turn) % top, axis=1)


def shares(amount, total, most, skew, full):
    loads = [(1 << 20) // math.isqrt(grade ** skew) + 1 for grade in range(1, amount + 1)]
    largest = most if full else min(most, max(-(-total // amount), total * loads[0] // sum(loads)))
    least = 1 if total - largest >= amount - 1 else 0
    given, spare = [largest] + [least] * (amount - 1), total - largest - least * (amount - 1)
    while spare > 0:
        free = [i for i in range(1, amount) if given[i] < largest] or [i for i in range(1, amount) if given[i] < most]
        whole, remaining = sum([loads[i] for i in free]), spare
        for i in free:
            extra = min(most - given[i], max(1, remaining * loads[i] // whole), spare)
            given[i] = given[i] + extra
            spare = spare - extra
    return np.array(given)


def normal_values(key, shape, scale, most, pieces=(), held_as=jnp.bfloat16):
    gain = levels(key, shape, pieces, -0.22, 0.18) if pieces else 1.0
    values = jax.random.normal(key, shape, jnp.float32) * scale * gain
    return jnp.minimum(jnp.maximum(values, -most), most).astype(held_as)


def setup_inputs(seed: int = 0) -> dict:
    arg_keys = jax.random.split(jax.random.key(seed), 9)
    cand_x = normal_values(arg_keys[0], (CANDS, D), 1.0, 6.0, ((0, 128),))
    cand_user_keys = jax.random.split(jax.random.fold_in(arg_keys[1], 1), CANDS // CAND_DEV)
    cand_user_turns = jax.random.permutation(jax.random.fold_in(arg_keys[1], 3), CANDS // CAND_DEV)
    cand_user = jax.vmap(lambda own, number: deal_out(jax.random.fold_in(arg_keys[1], 2), own, number, CAND_DEV, USERS, 1, CAP, 2))(cand_user_keys, cand_user_turns).reshape((CANDS, 1))
    visible = place_ends(jax.random.randint(arg_keys[2], (CANDS,), 1, HB + 1), jax.random.fold_in(arg_keys[2], 1), 1, HB).astype(jnp.int32)
    hist_len = place_ends(jax.random.randint(arg_keys[3], (USERS,), 1, HIST + 1), jax.random.fold_in(arg_keys[3], 1), 1, HIST).astype(jnp.int32)
    kv_cache = normal_values(arg_keys[4], (USERS, HIST, 2 * D), 1.0, 6.0, ((0, 16), (1, 8)))
    w_in = normal_values(arg_keys[5], (D, 2 * D), D ** -0.5, 0.1875)
    w_out = normal_values(arg_keys[6], (D, D), D ** -0.5, 0.1875)
    ln_gain = jnp.clip(1.0 + 0.18 * jax.random.normal(arg_keys[7], (D,), jnp.float32), 0.1, 1.9)
    return dict(cand_x=cand_x, cand_user=cand_user, visible=visible, hist_len=hist_len, kv_cache=kv_cache, w_in=w_in, w_out=w_out, ln_gain=ln_gain)


def reference(cand_x, cand_user, visible, hist_len, kv_cache, w_in, w_out, ln_gain):
    width = cand_x.shape[1]
    head_size = width // HEADS
    scale = 1.0 / math.sqrt(head_size)
    hidden = jax.nn.silu(jnp.dot(cand_x, w_in, preferred_element_type=jnp.float32))
    queries = hidden[:, :width].astype(jnp.bfloat16)
    gate = hidden[:, width:].astype(jnp.bfloat16)
    owner = cand_user[:, 0].astype(jnp.int32)
    order = jnp.argsort(owner, stable=True).astype(jnp.int32)
    sorted_rows = queries[order]
    sorted_owner = owner[order]
    sorted_vis = visible[order]
    block_rows = min(512, CANDS)
    positions = jnp.arange(HIST, dtype=jnp.int32).astype(jnp.float32)

    def one_block(packed):
        rows_part, owner_part, vis_part = packed
        query_heads = rows_part.astype(jnp.float32).reshape(block_rows, HEADS, head_size)

        def per_user(user_id, partial_value):
            history = lax.dynamic_index_in_dim(kv_cache, user_id, 0, keepdims=False)
            keys = history[:, :width].astype(jnp.float32).reshape(HIST, HEADS, head_size)
            values = history[:, width:].astype(jnp.float32).reshape(HIST, HEADS, head_size)
            limit = jnp.minimum(hist_len[user_id].astype(jnp.float32), BLK * vis_part.astype(jnp.float32))
            limit = jnp.where(owner_part == user_id, limit, jnp.float32(0.0))
            scores = jnp.einsum('bhd,nhd->hbn', query_heads, keys)
            visible_mask = (positions[None, :] < limit[:, None]).astype(jnp.float32)
            weights = (jax.nn.silu(scores * scale) * visible_mask[None]).astype(jnp.bfloat16)
            weights = lax.optimization_barrier(weights).astype(jnp.float32)
            mixed = jnp.einsum('hbn,nhd->bhd', weights, values)
            return partial_value + mixed.reshape(block_rows, width)
        first_user = owner_part[0].astype(jnp.int32)
        last_user = owner_part[block_rows - 1].astype(jnp.int32) + 1
        return lax.fori_loop(first_user, last_user, per_user, jnp.zeros((block_rows, width), jnp.float32))
    blocks = lax.map(one_block, (sorted_rows.reshape(-1, block_rows, width), sorted_owner.reshape(-1, block_rows), sorted_vis.reshape(-1, block_rows)))
    attn_sorted = blocks.reshape(CANDS, width)
    attn = jnp.zeros_like(attn_sorted).at[order].set(attn_sorted)
    mean_row = lax.optimization_barrier(jnp.mean(attn, axis=1, keepdims=True))
    centered = attn - mean_row
    variance = lax.optimization_barrier(jnp.mean(centered * centered, axis=1, keepdims=True))
    normed = (centered * lax.rsqrt(variance + 1e-06) * ln_gain.astype(jnp.float32)).astype(jnp.bfloat16)
    mixed_rows = (normed.astype(jnp.float32) * gate.astype(jnp.float32)).astype(jnp.bfloat16)
    projected = jnp.dot(mixed_rows, w_out, preferred_element_type=jnp.float32)
    return (cand_x.astype(jnp.float32) + projected).astype(jnp.bfloat16)
```

```python
import functools
import math

import jax
import jax.numpy as jnp
from jax import lax
from jax.experimental import pallas as pl
from jax.experimental.pallas import tpu as pltpu
from jax.sharding import PartitionSpec as P

HEADS = 8
BLK = 128
GATHER_CHUNKS = 2
SUB_ROWS = 256

norm_eps = 1e-06


def attend_kernel(seg_rows, chunk_rows, skip_own, base_ref, q_ref, lim_ref, kv_ref, acc_ref, o_ref):
    k = pl.program_id(0)
    me = base_ref[0]
    width = q_ref.shape[1]
    head_size = width // HEADS
    tk = kv_ref.shape[0]
    rows = q_ref.shape[0]
    half_scale = 0.5 / math.sqrt(head_size)

    @pl.when(k == 0)
    def _():
        o_ref[...] = acc_ref[...]

    if skip_own:
        start = k * seg_rows + base_ref[1]
        run = k != me
    else:
        start = me * seg_rows + k * tk
        run = k >= 0

    @pl.when(run)
    def _():
        def sub(r, carry):
            r0 = pl.multiple_of(r * SUB_ROWS, SUB_ROWS)
            lim = lim_ref[pl.ds(r0, SUB_ROWS), :]
            pos = start + lax.broadcasted_iota(jnp.int32, (SUB_ROWS, tk), 1)
            vis = pos < lim
            for h in range(HEADS):
                cols = slice(h * head_size, (h + 1) * head_size)
                qh = q_ref[pl.ds(r0, SUB_ROWS), cols]
                kh = kv_ref[:, cols]
                s = lax.dot_general(
                    qh, kh, (((1,), (1,)), ((), ())), preferred_element_type=jnp.float32
                )
                t = s * half_scale
                w = jnp.where(vis, t + t * jnp.tanh(t), 0.0).astype(jnp.bfloat16)
                vh = kv_ref[:, width + h * head_size : width + (h + 1) * head_size]
                o_ref[pl.ds(r0, SUB_ROWS), cols] += jnp.dot(
                    w, vh, preferred_element_type=jnp.float32
                )
            return carry

        lax.fori_loop(0, rows // SUB_ROWS, sub, 0)


def attend(queries, limits, kv, acc, base, seg_rows, skip_own):
    rows, width = queries.shape
    kv_rows = kv.shape[0]
    tk = seg_rows // GATHER_CHUNKS if skip_own else seg_rows
    steps = kv_rows // tk
    kernel = functools.partial(attend_kernel, seg_rows, tk, skip_own)
    flops = 4 * rows * kv_rows * width
    return pl.pallas_call(
        kernel,
        out_shape=jax.ShapeDtypeStruct((rows, width), jnp.float32),
        grid_spec=pltpu.PrefetchScalarGridSpec(
            num_scalar_prefetch=1,
            grid=(steps,),
            in_specs=[
                pl.BlockSpec((rows, width), lambda k, b: (0, 0)),
                pl.BlockSpec((rows, 1), lambda k, b: (0, 0)),
                pl.BlockSpec((tk, 2 * width), lambda k, b: (k, 0)),
                pl.BlockSpec((rows, width), lambda k, b: (0, 0)),
            ],
            out_specs=pl.BlockSpec((rows, width), lambda k, b: (0, 0)),
        ),
        input_output_aliases={4: 0},
        compiler_params=pltpu.CompilerParams(
            dimension_semantics=("arbitrary",), vmem_limit_bytes=60 * 1024 * 1024
        ),
        cost_estimate=pl.CostEstimate(
            flops=flops,
            transcendentals=rows * kv_rows * HEADS,
            bytes_accessed=kv_rows * 2 * width * 2 + rows * width * 10,
        ),
    )(base, queries, limits, kv, acc)


def per_device(cand_x, cand_user, visible, hist_len, kv_cache, w_in, w_out, ln_gain):
    rows, width = cand_x.shape
    columns = lax.axis_size("cand")
    capacity = 2 * rows // columns
    slots = columns * capacity
    hidden = jax.nn.silu(jnp.dot(cand_x, w_in, preferred_element_type=jnp.float32))
    queries = hidden[:, :width].astype(jnp.bfloat16)
    gate = hidden[:, width:].astype(jnp.bfloat16)
    owner = cand_user[:, 0]
    onehot = (owner[:, None] == jnp.arange(columns, dtype=jnp.int32)[None, :]).astype(jnp.int32)
    earlier = jnp.cumsum(onehot, axis=0) - onehot
    slot_of = owner * capacity + jnp.sum(earlier * onehot, axis=1)
    send_rows = jnp.zeros((slots, width), jnp.bfloat16).at[slot_of].set(queries)
    send_vis = jnp.zeros((slots,), jnp.bfloat16).at[slot_of].set(visible.astype(jnp.bfloat16))
    got_rows, got_vis = (
        lax.all_to_all(
            send_rows.reshape(columns, capacity, width),
            "cand",
            split_axis=0,
            concat_axis=0,
            tiled=True,
        ),
        lax.all_to_all(
            send_vis.reshape(columns, capacity), "cand", split_axis=0, concat_axis=0, tiled=True
        ),
    )
    got_rows = got_rows.reshape(slots, width)
    got_vis = got_vis.reshape(slots)
    user_length = hist_len[0].astype(jnp.float32)
    limits = jnp.minimum(user_length, BLK * got_vis.astype(jnp.float32)).astype(jnp.int32)
    limits = limits.reshape(slots, 1)

    segment = kv_cache[0]
    seg_rows = segment.shape[0]
    me = lax.axis_index("user").astype(jnp.int32)
    chunk_rows = seg_rows // GATHER_CHUNKS
    acc = jnp.zeros((slots, width), jnp.float32)
    acc = attend(got_rows, limits, segment, acc, jnp.stack([me, jnp.int32(0)]), seg_rows, False)
    for c in range(GATHER_CHUNKS):
        piece = lax.all_gather(
            segment[c * chunk_rows : (c + 1) * chunk_rows], "user", axis=0, tiled=True
        )
        acc = attend(
            got_rows, limits, piece, acc, jnp.stack([me, jnp.int32(c * chunk_rows)]), seg_rows, True
        )
    partial_value = acc
    mean_row = jnp.mean(partial_value, axis=1, keepdims=True)
    centered = partial_value - mean_row
    variance = jnp.mean(centered * centered, axis=1, keepdims=True)
    normed = (centered * lax.rsqrt(variance + norm_eps) * ln_gain).astype(jnp.bfloat16)
    returned = lax.all_to_all(
        normed.reshape(columns, capacity, width), "cand", split_axis=0, concat_axis=0, tiled=True
    ).reshape(slots, width)
    home_rows = returned[slot_of]
    mixed_rows = (home_rows.astype(jnp.float32) * gate.astype(jnp.float32)).astype(jnp.bfloat16)
    projected = jnp.dot(mixed_rows, w_out, preferred_element_type=jnp.float32)
    return (cand_x.astype(jnp.float32) + projected).astype(jnp.bfloat16)


def solution(mesh):
    in_specs = (
        P(("user", "cand"), None),
        P(("user", "cand"), None),
        P(("user", "cand")),
        P("cand"),
        P("cand", "user", None),
        P(),
        P(),
        P(),
    )
    out_specs = P(("user", "cand"), None)
    return jax.shard_map(
        per_device, mesh=mesh, in_specs=in_specs, out_specs=out_specs, check_vma=False
    )
```

```python
import functools
import math

import jax
import jax.numpy as jnp
from jax import lax
from jax.experimental import pallas as pl
from jax.experimental.pallas import tpu as pltpu
from jax.sharding import PartitionSpec as P

HEADS = 8
BLK = 128
SUB_ROWS = 1024

norm_eps = 1e-06


def attend_kernel(seg_rows, skip_own, base_ref, q_ref, lim_ref, kv_ref, acc_ref, o_ref):
    k = pl.program_id(0)
    me = base_ref[0]
    width = q_ref.shape[1]
    head_size = width // HEADS
    tk = kv_ref.shape[0]
    rows = q_ref.shape[0]
    half_scale = 0.5 / math.sqrt(head_size)

    @pl.when(k == 0)
    def _():
        o_ref[...] = acc_ref[...]

    if skip_own:
        start = k * seg_rows
        run = k != me
    else:
        start = me * seg_rows + k * tk
        run = k >= 0

    @pl.when(run)
    def _():
        def sub(r, carry):
            r0 = pl.multiple_of(r * SUB_ROWS, SUB_ROWS)
            lim = lim_ref[pl.ds(r0, SUB_ROWS), :]
            pos = start + lax.broadcasted_iota(jnp.int32, (SUB_ROWS, tk), 1)
            vis = pos < lim
            for h in range(HEADS):
                cols = slice(h * head_size, (h + 1) * head_size)
                qh = q_ref[pl.ds(r0, SUB_ROWS), cols]
                kh = kv_ref[:, cols]
                s = lax.dot_general(
                    qh, kh, (((1,), (1,)), ((), ())), preferred_element_type=jnp.float32
                )
                t = s * half_scale
                w = jnp.where(vis, t + t * jnp.tanh(t), 0.0).astype(jnp.bfloat16)
                vh = kv_ref[:, width + h * head_size : width + (h + 1) * head_size]
                o_ref[pl.ds(r0, SUB_ROWS), cols] += jnp.dot(
                    w, vh, preferred_element_type=jnp.float32
                )
            return carry

        lax.fori_loop(0, rows // SUB_ROWS, sub, 0)


def attend(queries, limits, kv, acc, base, seg_rows, skip_own):
    rows, width = queries.shape
    kv_rows = kv.shape[0]
    tk = seg_rows
    steps = kv_rows // tk
    kernel = functools.partial(attend_kernel, seg_rows, skip_own)
    flops = 4 * rows * kv_rows * width
    return pl.pallas_call(
        kernel,
        out_shape=jax.ShapeDtypeStruct((rows, width), jnp.float32),
        grid_spec=pltpu.PrefetchScalarGridSpec(
            num_scalar_prefetch=1,
            grid=(steps,),
            in_specs=[
                pl.BlockSpec((rows, width), lambda k, b: (0, 0)),
                pl.BlockSpec((rows, 1), lambda k, b: (0, 0)),
                pl.BlockSpec((tk, 2 * width), lambda k, b: (k, 0)),
                pl.BlockSpec((rows, width), lambda k, b: (0, 0)),
            ],
            out_specs=pl.BlockSpec((rows, width), lambda k, b: (0, 0)),
        ),
        input_output_aliases={4: 0},
        compiler_params=pltpu.CompilerParams(
            dimension_semantics=("arbitrary",), vmem_limit_bytes=60 * 1024 * 1024
        ),
        cost_estimate=pl.CostEstimate(
            flops=flops,
            transcendentals=rows * kv_rows * HEADS,
            bytes_accessed=kv_rows * 2 * width * 2 + rows * width * 10,
        ),
    )(base, queries, limits, kv, acc)


def per_device(cand_x, cand_user, visible, hist_len, kv_cache, w_in, w_out, ln_gain):
    rows, width = cand_x.shape
    columns = lax.axis_size("cand")
    capacity = 2 * rows // columns
    slots = columns * capacity
    hidden = jax.nn.silu(jnp.dot(cand_x, w_in, preferred_element_type=jnp.float32))
    queries = hidden[:, :width].astype(jnp.bfloat16)
    gate = hidden[:, width:].astype(jnp.bfloat16)
    owner = cand_user[:, 0]
    onehot = (owner[:, None] == jnp.arange(columns, dtype=jnp.int32)[None, :]).astype(jnp.int32)
    earlier = jnp.cumsum(onehot, axis=0) - onehot
    slot_of = owner * capacity + jnp.sum(earlier * onehot, axis=1)
    send_rows = jnp.zeros((slots, width), jnp.bfloat16).at[slot_of].set(queries)
    send_vis = jnp.zeros((slots,), jnp.bfloat16).at[slot_of].set(visible.astype(jnp.bfloat16))
    got_rows, got_vis = (
        lax.all_to_all(
            send_rows.reshape(columns, capacity, width),
            "cand",
            split_axis=0,
            concat_axis=0,
            tiled=True,
        ),
        lax.all_to_all(
            send_vis.reshape(columns, capacity), "cand", split_axis=0, concat_axis=0, tiled=True
        ),
    )
    got_rows = got_rows.reshape(slots, width)
    got_vis = got_vis.reshape(slots)
    user_length = hist_len[0].astype(jnp.float32)
    limits = jnp.minimum(user_length, BLK * got_vis.astype(jnp.float32)).astype(jnp.int32)
    limits = limits.reshape(slots, 1)

    segment = kv_cache[0]
    seg_rows = segment.shape[0]
    me = lax.axis_index("user").astype(jnp.int32)
    acc = jnp.zeros((slots, width), jnp.float32)
    acc = attend(got_rows, limits, segment, acc, me.reshape(1), seg_rows, False)
    history = lax.all_gather(segment, "user", axis=0, tiled=True)
    acc = attend(got_rows, limits, history, acc, me.reshape(1), seg_rows, True)
    partial_value = acc
    mean_row = jnp.mean(partial_value, axis=1, keepdims=True)
    centered = partial_value - mean_row
    variance = jnp.mean(centered * centered, axis=1, keepdims=True)
    normed = (centered * lax.rsqrt(variance + norm_eps) * ln_gain).astype(jnp.bfloat16)
    returned = lax.all_to_all(
        normed.reshape(columns, capacity, width), "cand", split_axis=0, concat_axis=0, tiled=True
    ).reshape(slots, width)
    home_rows = returned[slot_of]
    mixed_rows = (home_rows.astype(jnp.float32) * gate.astype(jnp.float32)).astype(jnp.bfloat16)
    projected = jnp.dot(mixed_rows, w_out, preferred_element_type=jnp.float32)
    return (cand_x.astype(jnp.float32) + projected).astype(jnp.bfloat16)


def solution(mesh):
    in_specs = (
        P(("user", "cand"), None),
        P(("user", "cand"), None),
        P(("user", "cand")),
        P("cand"),
        P("cand", "user", None),
        P(),
        P(),
        P(),
    )
    out_specs = P(("user", "cand"), None)
    return jax.shard_map(
        per_device, mesh=mesh, in_specs=in_specs, out_specs=out_specs, check_vma=False
    )
```

```python
import functools
import math

import jax
import jax.numpy as jnp
from jax import lax
from jax.experimental import pallas as pl
from jax.experimental.pallas import tpu as pltpu
from jax.sharding import PartitionSpec as P

HEADS = 8
BLK = 128
SUB_ROWS = 1024

norm_eps = 1e-06


def attend_kernel(seg_rows, skip_own, final, base_ref, q_ref, lim_ref, kv_ref, acc_ref, *rest):
    if final:
        gain_ref, o_ref, total = rest
    else:
        (o_ref,) = rest
        total = o_ref
    k = pl.program_id(0)
    last = pl.num_programs(0) - 1
    me = base_ref[0]
    rows, width = q_ref.shape
    head_size = width // HEADS
    tk = kv_ref.shape[0]
    half_scale = 0.5 / math.sqrt(head_size)

    @pl.when(k == 0)
    def _():
        total[...] = acc_ref[...]

    if skip_own:
        start = k * seg_rows
        run = k != me
    elif final:
        start = k * seg_rows
        run = k >= 0
    else:
        start = me * seg_rows + k * tk
        run = k >= 0

    @pl.when(run)
    def _():
        pos = start + lax.broadcasted_iota(jnp.int32, (rows, tk), 1)
        vis = pos < lim_ref[...]
        for h in range(HEADS):
            cols = slice(h * head_size, (h + 1) * head_size)
            s = lax.dot_general(
                q_ref[:, cols],
                kv_ref[:, cols],
                (((1,), (1,)), ((), ())),
                preferred_element_type=jnp.float32,
            )
            t = s * half_scale
            w = jnp.where(vis, t + t * jnp.tanh(t), 0.0).astype(jnp.bfloat16)
            vh = kv_ref[:, width + h * head_size : width + (h + 1) * head_size]
            total[:, cols] += jnp.dot(w, vh, preferred_element_type=jnp.float32)

    if final:

        @pl.when(k == last)
        def _():
            value = total[...]
            mean_row = jnp.mean(value, axis=1, keepdims=True)
            centered = value - mean_row
            variance = jnp.mean(centered * centered, axis=1, keepdims=True)
            scale_row = lax.rsqrt(variance + norm_eps)
            o_ref[...] = (centered * scale_row * gain_ref[...]).astype(o_ref.dtype)


def attend(queries, limits, kv, acc, base, seg_rows, skip_own, gain=None):
    rows, width = queries.shape
    kv_rows = kv.shape[0]
    tk = seg_rows
    steps = kv_rows // tk
    final = gain is not None
    kernel = functools.partial(attend_kernel, seg_rows, skip_own, final)
    flops = 4 * rows * kv_rows * width
    in_specs = [
        pl.BlockSpec((rows, width), lambda k, b: (0, 0)),
        pl.BlockSpec((rows, 1), lambda k, b: (0, 0)),
        pl.BlockSpec((tk, 2 * width), lambda k, b: (k, 0)),
        pl.BlockSpec((rows, width), lambda k, b: (0, 0)),
    ]
    operands = [base, queries, limits, kv, acc]
    if final:
        in_specs.append(pl.BlockSpec((1, width), lambda k, b: (0, 0)))
        operands.append(gain.reshape(1, width))
        out_dtype = jnp.bfloat16
        scratch = [pltpu.VMEM((rows, width), jnp.float32)]
        aliases = {}
    else:
        out_dtype = jnp.float32
        scratch = []
        aliases = {4: 0}
    return pl.pallas_call(
        kernel,
        out_shape=jax.ShapeDtypeStruct((rows, width), out_dtype),
        grid_spec=pltpu.PrefetchScalarGridSpec(
            num_scalar_prefetch=1,
            grid=(steps,),
            in_specs=in_specs,
            out_specs=pl.BlockSpec((rows, width), lambda k, b: (0, 0)),
            scratch_shapes=scratch,
        ),
        input_output_aliases=aliases,
        compiler_params=pltpu.CompilerParams(
            dimension_semantics=("arbitrary",), vmem_limit_bytes=60 * 1024 * 1024
        ),
        cost_estimate=pl.CostEstimate(
            flops=flops,
            transcendentals=rows * kv_rows * HEADS,
            bytes_accessed=kv_rows * 2 * width * 2 + rows * width * 10,
        ),
    )(*operands)


def per_device(cand_x, cand_user, visible, hist_len, kv_cache, w_in, w_out, ln_gain):
    rows, width = cand_x.shape
    columns = lax.axis_size("cand")
    capacity = 2 * rows // columns
    slots = columns * capacity
    hidden = jax.nn.silu(jnp.dot(cand_x, w_in, preferred_element_type=jnp.float32))
    queries = hidden[:, :width].astype(jnp.bfloat16)
    gate = hidden[:, width:].astype(jnp.bfloat16)
    owner = cand_user[:, 0]
    onehot = (owner[:, None] == jnp.arange(columns, dtype=jnp.int32)[None, :]).astype(jnp.int32)
    earlier = jnp.cumsum(onehot, axis=0) - onehot
    slot_of = owner * capacity + jnp.sum(earlier * onehot, axis=1)
    send_rows = jnp.zeros((slots, width), jnp.bfloat16).at[slot_of].set(queries)
    send_vis = jnp.zeros((slots,), jnp.bfloat16).at[slot_of].set(visible.astype(jnp.bfloat16))
    send_rows = send_rows.reshape(columns, 2, capacity // 2, width)
    send_vis = send_vis.reshape(columns, 2, capacity // 2)
    half_slots = slots // 2
    user_length = hist_len[0].astype(jnp.float32)
    segment = kv_cache[0]
    seg_rows = segment.shape[0]
    me = lax.axis_index("user").astype(jnp.int32).reshape(1)
    halves = []
    for half in range(2):
        got_rows = lax.all_to_all(
            send_rows[:, half], "cand", split_axis=0, concat_axis=0, tiled=True
        ).reshape(half_slots, width)
        got_vis = lax.all_to_all(
            send_vis[:, half], "cand", split_axis=0, concat_axis=0, tiled=True
        ).reshape(half_slots)
        limits = jnp.minimum(user_length, BLK * got_vis.astype(jnp.float32)).astype(jnp.int32)
        limits = limits.reshape(half_slots, 1)
        acc = jnp.zeros((half_slots, width), jnp.float32)
        halves.append((got_rows, limits, acc))
    history = lax.all_gather(segment, "user", axis=0, tiled=True)
    returned = []
    for got_rows, limits, acc in halves:
        normed = attend(got_rows, limits, history, acc, me, seg_rows, False, ln_gain)
        back = lax.all_to_all(
            normed.reshape(columns, capacity // 2, width),
            "cand",
            split_axis=0,
            concat_axis=0,
            tiled=True,
        )
        returned.append(back)
    returned = jnp.stack(returned, axis=1).reshape(slots, width)
    home_rows = returned[slot_of]
    mixed_rows = (home_rows.astype(jnp.float32) * gate.astype(jnp.float32)).astype(jnp.bfloat16)
    projected = jnp.dot(mixed_rows, w_out, preferred_element_type=jnp.float32)
    return (cand_x.astype(jnp.float32) + projected).astype(jnp.bfloat16)


def solution(mesh):
    in_specs = (
        P(("user", "cand"), None),
        P(("user", "cand"), None),
        P(("user", "cand")),
        P("cand"),
        P("cand", "user", None),
        P(),
        P(),
        P(),
    )
    out_specs = P(("user", "cand"), None)
    return jax.shard_map(
        per_device, mesh=mesh, in_specs=in_specs, out_specs=out_specs, check_vma=False
    )
```

```python
import functools
import math

import jax
import jax.numpy as jnp
from jax import lax
from jax.experimental import pallas as pl
from jax.experimental.pallas import tpu as pltpu
from jax.sharding import PartitionSpec as P

HEADS = 8
BLK = 128
SUB_ROWS = 1024

norm_eps = 1e-06


def attend_kernel(seg_rows, skip_own, base_ref, q_ref, lim_ref, kv_ref, acc_ref, o_ref):
    k = pl.program_id(0)
    me = base_ref[0]
    width = q_ref.shape[1]
    head_size = width // HEADS
    tk = kv_ref.shape[0]
    rows = q_ref.shape[0]
    half_scale = 0.5 / math.sqrt(head_size)

    @pl.when(k == 0)
    def _():
        o_ref[...] = acc_ref[...]

    if skip_own:
        start = k * seg_rows
        run = k != me
    else:
        start = me * seg_rows + k * tk
        run = k >= 0

    @pl.when(run)
    def _():
        def sub(r, carry):
            r0 = pl.multiple_of(r * SUB_ROWS, SUB_ROWS)
            lim = lim_ref[pl.ds(r0, SUB_ROWS), :]
            pos = start + lax.broadcasted_iota(jnp.int32, (SUB_ROWS, tk), 1)
            vis = pos < lim
            for h in range(HEADS):
                cols = slice(h * head_size, (h + 1) * head_size)
                qh = q_ref[pl.ds(r0, SUB_ROWS), cols]
                kh = kv_ref[:, cols]
                s = lax.dot_general(
                    qh, kh, (((1,), (1,)), ((), ())), preferred_element_type=jnp.float32
                )
                t = s * half_scale
                w = jnp.where(vis, t + t * jnp.tanh(t), 0.0).astype(jnp.bfloat16)
                vh = kv_ref[:, width + h * head_size : width + (h + 1) * head_size]
                o_ref[pl.ds(r0, SUB_ROWS), cols] += jnp.dot(
                    w, vh, preferred_element_type=jnp.float32
                )
            return carry

        lax.fori_loop(0, rows // SUB_ROWS, sub, 0)


def attend(queries, limits, kv, acc, base, seg_rows, skip_own):
    rows, width = queries.shape
    kv_rows = kv.shape[0]
    tk = seg_rows
    steps = kv_rows // tk
    kernel = functools.partial(attend_kernel, seg_rows, skip_own)
    flops = 4 * rows * kv_rows * width
    return pl.pallas_call(
        kernel,
        out_shape=jax.ShapeDtypeStruct((rows, width), jnp.float32),
        grid_spec=pltpu.PrefetchScalarGridSpec(
            num_scalar_prefetch=1,
            grid=(steps,),
            in_specs=[
                pl.BlockSpec((rows, width), lambda k, b: (0, 0)),
                pl.BlockSpec((rows, 1), lambda k, b: (0, 0)),
                pl.BlockSpec((tk, 2 * width), lambda k, b: (k, 0)),
                pl.BlockSpec((rows, width), lambda k, b: (0, 0)),
            ],
            out_specs=pl.BlockSpec((rows, width), lambda k, b: (0, 0)),
        ),
        input_output_aliases={4: 0},
        compiler_params=pltpu.CompilerParams(
            dimension_semantics=("arbitrary",), vmem_limit_bytes=60 * 1024 * 1024
        ),
        cost_estimate=pl.CostEstimate(
            flops=flops,
            transcendentals=rows * kv_rows * HEADS,
            bytes_accessed=kv_rows * 2 * width * 2 + rows * width * 10,
        ),
    )(base, queries, limits, kv, acc)


def fused_kernel(peers, key_rows, q_ref, lim_ref, gain_ref, hist_hbm, out_hbm,
                 kv_buf, kv_sem, acc, normed, send_sem, recv_sem, local_sem):
    me = lax.axis_index("cand")
    uid = lax.axis_index("user")
    rows, width = q_ref.shape
    half_rows = rows // 2
    blk = half_rows // peers
    cap = 2 * blk
    head_size = width // HEADS
    half_scale = 0.5 / math.sqrt(head_size)
    segments = hist_hbm.shape[0] // key_rows
    steps = 2 * segments

    barrier = pltpu.get_barrier_semaphore()
    for j in range(1, peers):
        pl.semaphore_signal(
            barrier, inc=1, device_id=(uid, lax.rem(me + j, peers)), device_id_type=pl.DeviceIdType.MESH
        )
    pl.semaphore_wait(barrier, peers - 1)

    def kv_copy(s, slot):
        k = lax.rem(s, segments)
        return pltpu.make_async_copy(
            hist_hbm.at[pl.ds(pl.multiple_of(k * key_rows, key_rows), key_rows)],
            kv_buf.at[slot],
            kv_sem.at[slot],
        )

    def remote(half, j):
        p = lax.rem(me + j, peers)
        return pltpu.make_async_remote_copy(
            src_ref=normed.at[half, pl.ds(pl.multiple_of(p * blk, blk), blk)],
            dst_ref=out_hbm.at[pl.ds(pl.multiple_of(me * cap + half * blk, blk), blk)],
            send_sem=send_sem.at[half, j],
            recv_sem=recv_sem.at[half, j],
            device_id=(uid, p),
            device_id_type=pl.DeviceIdType.MESH,
        )

    def incoming(half, j):
        src = lax.rem(me + peers - j, peers)
        return pltpu.make_async_remote_copy(
            src_ref=normed.at[half, pl.ds(pl.multiple_of(me * blk, blk), blk)],
            dst_ref=out_hbm.at[pl.ds(pl.multiple_of(src * cap + half * blk, blk), blk)],
            send_sem=send_sem.at[half, j],
            recv_sem=recv_sem.at[half, j],
            device_id=(uid, src),
            device_id_type=pl.DeviceIdType.MESH,
        )

    def local(half):
        return pltpu.make_async_copy(
            normed.at[half, pl.ds(pl.multiple_of(me * blk, blk), blk)],
            out_hbm.at[pl.ds(pl.multiple_of(me * cap + half * blk, blk), blk)],
            local_sem.at[half],
        )

    kv_copy(0, 0).start()

    def step(s, carry):
        slot = lax.rem(s, 2)
        half = s // segments
        k = lax.rem(s, segments)
        kv_copy(s, slot).wait()

        @pl.when(s + 1 < steps)
        def _():
            kv_copy(s + 1, 1 - slot).start()

        @pl.when(k == 0)
        def _():
            acc[...] = jnp.zeros_like(acc)

        q_rows = pl.ds(pl.multiple_of(half * half_rows, half_rows), half_rows)
        pos = k * key_rows + lax.broadcasted_iota(jnp.int32, (half_rows, key_rows), 1)
        vis = pos < lim_ref[q_rows, :]
        block = kv_buf.at[slot]
        for h in range(HEADS):
            cols = slice(h * head_size, (h + 1) * head_size)
            scores = lax.dot_general(
                q_ref[q_rows, cols],
                block[:, cols],
                (((1,), (1,)), ((), ())),
                preferred_element_type=jnp.float32,
            )
            t = scores * half_scale
            w = jnp.where(vis, t + t * jnp.tanh(t), 0.0).astype(jnp.bfloat16)
            vh = block[:, width + h * head_size : width + (h + 1) * head_size]
            acc[:, cols] += jnp.dot(w, vh, preferred_element_type=jnp.float32)

        @pl.when(k == segments - 1)
        def _():
            value = acc[...]
            mean_row = jnp.mean(value, axis=1, keepdims=True)
            centered = value - mean_row
            variance = jnp.mean(centered * centered, axis=1, keepdims=True)
            scale_row = lax.rsqrt(variance + norm_eps)
            normed[half] = (centered * scale_row * gain_ref[...]).astype(jnp.bfloat16)
            local(half).start()
            for j in range(1, peers):
                remote(half, j).start()

        return carry

    lax.fori_loop(0, steps, step, 0)

    for half in range(2):
        local(half).wait()
        for j in range(1, peers):
            remote(half, j).wait_send()
            incoming(half, j).wait_recv()


def attend_and_return(queries, limits, history, gain, peers, key_rows):
    rows, width = queries.shape
    kernel = functools.partial(fused_kernel, peers, key_rows)
    return pl.pallas_call(
        kernel,
        out_shape=jax.ShapeDtypeStruct((rows, width), jnp.bfloat16),
        in_specs=[
            pl.BlockSpec(memory_space=pltpu.VMEM),
            pl.BlockSpec(memory_space=pltpu.VMEM),
            pl.BlockSpec(memory_space=pltpu.VMEM),
            pl.BlockSpec(memory_space=pl.ANY),
        ],
        out_specs=pl.BlockSpec(memory_space=pl.ANY),
        scratch_shapes=[
            pltpu.VMEM((2, key_rows, 2 * width), jnp.bfloat16),
            pltpu.SemaphoreType.DMA((2,)),
            pltpu.VMEM((rows // 2, width), jnp.float32),
            pltpu.VMEM((2, rows // 2, width), jnp.bfloat16),
            pltpu.SemaphoreType.DMA((2, peers)),
            pltpu.SemaphoreType.DMA((2, peers)),
            pltpu.SemaphoreType.DMA((2,)),
        ],
        compiler_params=pltpu.CompilerParams(
            collective_id=0, has_side_effects=True, vmem_limit_bytes=60 * 1024 * 1024
        ),
        cost_estimate=pl.CostEstimate(
            flops=8 * rows * history.shape[0] * width,
            transcendentals=rows * history.shape[0] * HEADS,
            bytes_accessed=2 * history.size * 2 + rows * width * 6,
        ),
    )(queries, limits, gain.reshape(1, width), history)


def per_device(cand_x, cand_user, visible, hist_len, kv_cache, w_in, w_out, ln_gain):
    rows, width = cand_x.shape
    columns = lax.axis_size("cand")
    capacity = 2 * rows // columns
    slots = columns * capacity
    hidden = jax.nn.silu(jnp.dot(cand_x, w_in, preferred_element_type=jnp.float32))
    queries = hidden[:, :width].astype(jnp.bfloat16)
    gate = hidden[:, width:].astype(jnp.bfloat16)
    owner = cand_user[:, 0]
    onehot = (owner[:, None] == jnp.arange(columns, dtype=jnp.int32)[None, :]).astype(jnp.int32)
    earlier = jnp.cumsum(onehot, axis=0) - onehot
    slot_of = owner * capacity + jnp.sum(earlier * onehot, axis=1)
    send_rows = jnp.zeros((slots, width), jnp.bfloat16).at[slot_of].set(queries)
    send_vis = jnp.zeros((slots,), jnp.bfloat16).at[slot_of].set(visible.astype(jnp.bfloat16))
    got_rows, got_vis = (
        lax.all_to_all(
            send_rows.reshape(columns, capacity, width),
            "cand",
            split_axis=0,
            concat_axis=0,
            tiled=True,
        ),
        lax.all_to_all(
            send_vis.reshape(columns, capacity), "cand", split_axis=0, concat_axis=0, tiled=True
        ),
    )
    got_rows = got_rows.reshape(slots, width)
    got_vis = got_vis.reshape(slots)
    user_length = hist_len[0].astype(jnp.float32)
    limits = jnp.minimum(user_length, BLK * got_vis.astype(jnp.float32)).astype(jnp.int32)
    halves = lambda x: jnp.swapaxes(x.reshape(columns, 2, capacity // 2, -1), 0, 1).reshape(slots, -1)
    segment = kv_cache[0]
    history = lax.all_gather(segment, "user", axis=0, tiled=True)
    returned = attend_and_return(
        halves(got_rows), halves(limits.reshape(slots, 1)), history, ln_gain, columns, segment.shape[0]
    )
    home_rows = returned[slot_of]
    mixed_rows = (home_rows.astype(jnp.float32) * gate.astype(jnp.float32)).astype(jnp.bfloat16)
    projected = jnp.dot(mixed_rows, w_out, preferred_element_type=jnp.float32)
    return (cand_x.astype(jnp.float32) + projected).astype(jnp.bfloat16)


def solution(mesh):
    in_specs = (
        P(("user", "cand"), None),
        P(("user", "cand"), None),
        P(("user", "cand")),
        P("cand"),
        P("cand", "user", None),
        P(),
        P(),
        P(),
    )
    out_specs = P(("user", "cand"), None)
    return jax.shard_map(
        per_device, mesh=mesh, in_specs=in_specs, out_specs=out_specs, check_vma=False
    )
```

```python
import functools
import math

import jax
import jax.numpy as jnp
from jax import lax
from jax.experimental import pallas as pl
from jax.experimental.pallas import tpu as pltpu
from jax.sharding import PartitionSpec as P

HEADS = 8
BLK = 128
SUB_ROWS = 1024

norm_eps = 1e-06


def attend_kernel(seg_rows, skip_own, base_ref, q_ref, lim_ref, kv_ref, acc_ref, o_ref):
    k = pl.program_id(0)
    me = base_ref[0]
    width = q_ref.shape[1]
    head_size = width // HEADS
    tk = kv_ref.shape[0]
    rows = q_ref.shape[0]
    half_scale = 0.5 / math.sqrt(head_size)

    @pl.when(k == 0)
    def _():
        o_ref[...] = acc_ref[...]

    if skip_own:
        start = k * seg_rows
        run = k != me
    else:
        start = me * seg_rows + k * tk
        run = k >= 0

    @pl.when(run)
    def _():
        def sub(r, carry):
            r0 = pl.multiple_of(r * SUB_ROWS, SUB_ROWS)
            lim = lim_ref[pl.ds(r0, SUB_ROWS), :]
            pos = start + lax.broadcasted_iota(jnp.int32, (SUB_ROWS, tk), 1)
            vis = pos < lim
            for h in range(HEADS):
                cols = slice(h * head_size, (h + 1) * head_size)
                qh = q_ref[pl.ds(r0, SUB_ROWS), cols]
                kh = kv_ref[:, cols]
                s = lax.dot_general(
                    qh, kh, (((1,), (1,)), ((), ())), preferred_element_type=jnp.float32
                )
                t = s * half_scale
                w = jnp.where(vis, t + t * jnp.tanh(t), 0.0).astype(jnp.bfloat16)
                vh = kv_ref[:, width + h * head_size : width + (h + 1) * head_size]
                o_ref[pl.ds(r0, SUB_ROWS), cols] += jnp.dot(
                    w, vh, preferred_element_type=jnp.float32
                )
            return carry

        lax.fori_loop(0, rows // SUB_ROWS, sub, 0)


def attend(queries, limits, kv, acc, base, seg_rows, skip_own):
    rows, width = queries.shape
    kv_rows = kv.shape[0]
    tk = seg_rows
    steps = kv_rows // tk
    kernel = functools.partial(attend_kernel, seg_rows, skip_own)
    flops = 4 * rows * kv_rows * width
    return pl.pallas_call(
        kernel,
        out_shape=jax.ShapeDtypeStruct((rows, width), jnp.float32),
        grid_spec=pltpu.PrefetchScalarGridSpec(
            num_scalar_prefetch=1,
            grid=(steps,),
            in_specs=[
                pl.BlockSpec((rows, width), lambda k, b: (0, 0)),
                pl.BlockSpec((rows, 1), lambda k, b: (0, 0)),
                pl.BlockSpec((tk, 2 * width), lambda k, b: (k, 0)),
                pl.BlockSpec((rows, width), lambda k, b: (0, 0)),
            ],
            out_specs=pl.BlockSpec((rows, width), lambda k, b: (0, 0)),
        ),
        input_output_aliases={4: 0},
        compiler_params=pltpu.CompilerParams(
            dimension_semantics=("arbitrary",), vmem_limit_bytes=60 * 1024 * 1024
        ),
        cost_estimate=pl.CostEstimate(
            flops=flops,
            transcendentals=rows * kv_rows * HEADS,
            bytes_accessed=kv_rows * 2 * width * 2 + rows * width * 10,
        ),
    )(base, queries, limits, kv, acc)


def fused_kernel(peers, key_rows, q_ref, lim_ref, gain_ref, hist_hbm, out_hbm,
                 kv_buf, kv_sem, acc, normed, send_sem, recv_sem, local_sem):
    me = lax.axis_index("cand")
    uid = lax.axis_index("user")
    rows, width = q_ref.shape
    half_rows = rows // 2
    blk = half_rows // peers
    cap = 2 * blk
    head_size = width // HEADS
    half_scale = 0.5 / math.sqrt(head_size)
    segments = hist_hbm.shape[0] // key_rows
    steps = 2 * segments

    barrier = pltpu.get_barrier_semaphore()
    for j in range(1, peers):
        pl.semaphore_signal(
            barrier, inc=1, device_id=(uid, lax.rem(me + j, peers)), device_id_type=pl.DeviceIdType.MESH
        )
    pl.semaphore_wait(barrier, peers - 1)

    def kv_copy(s, slot):
        k = lax.rem(s, segments)
        return pltpu.make_async_copy(
            hist_hbm.at[pl.ds(pl.multiple_of(k * key_rows, key_rows), key_rows)],
            kv_buf.at[slot],
            kv_sem.at[slot],
        )

    def remote(half, j):
        p = lax.rem(me + j, peers)
        return pltpu.make_async_remote_copy(
            src_ref=normed.at[half, pl.ds(pl.multiple_of(p * blk, blk), blk)],
            dst_ref=out_hbm.at[pl.ds(pl.multiple_of(me * cap + half * blk, blk), blk)],
            send_sem=send_sem.at[half, j],
            recv_sem=recv_sem.at[half, j],
            device_id=(uid, p),
            device_id_type=pl.DeviceIdType.MESH,
        )

    def incoming(half, j):
        src = lax.rem(me + peers - j, peers)
        return pltpu.make_async_remote_copy(
            src_ref=normed.at[half, pl.ds(pl.multiple_of(me * blk, blk), blk)],
            dst_ref=out_hbm.at[pl.ds(pl.multiple_of(src * cap + half * blk, blk), blk)],
            send_sem=send_sem.at[half, j],
            recv_sem=recv_sem.at[half, j],
            device_id=(uid, src),
            device_id_type=pl.DeviceIdType.MESH,
        )

    def local(half):
        return pltpu.make_async_copy(
            normed.at[half, pl.ds(pl.multiple_of(me * blk, blk), blk)],
            out_hbm.at[pl.ds(pl.multiple_of(me * cap + half * blk, blk), blk)],
            local_sem.at[half],
        )

    kv_copy(0, 0).start()

    def step(s, carry):
        slot = lax.rem(s, 2)
        half = s // segments
        k = lax.rem(s, segments)
        kv_copy(s, slot).wait()

        @pl.when(s + 1 < steps)
        def _():
            kv_copy(s + 1, 1 - slot).start()

        @pl.when(k == 0)
        def _():
            acc[...] = jnp.zeros_like(acc)

        q_rows = pl.ds(pl.multiple_of(half * half_rows, half_rows), half_rows)
        pos = k * key_rows + lax.broadcasted_iota(jnp.int32, (half_rows, key_rows), 1)
        vis = pos < lim_ref[q_rows, :]
        block = kv_buf.at[slot]
        for h in range(HEADS):
            cols = slice(h * head_size, (h + 1) * head_size)
            scores = lax.dot_general(
                q_ref[q_rows, cols],
                block[:, cols],
                (((1,), (1,)), ((), ())),
                preferred_element_type=jnp.float32,
            )
            t = scores * half_scale
            w = jnp.where(vis, t + t * jnp.tanh(t), 0.0).astype(jnp.bfloat16)
            vh = block[:, width + h * head_size : width + (h + 1) * head_size]
            acc[:, cols] += jnp.dot(w, vh, preferred_element_type=jnp.float32)

        @pl.when(k == segments - 1)
        def _():
            value = acc[...]
            mean_row = jnp.mean(value, axis=1, keepdims=True)
            centered = value - mean_row
            variance = jnp.mean(centered * centered, axis=1, keepdims=True)
            scale_row = lax.rsqrt(variance + norm_eps)
            normed[half] = (centered * scale_row * gain_ref[...]).astype(jnp.bfloat16)
            local(half).start()
            for j in range(1, peers):
                remote(half, j).start()

        return carry

    lax.fori_loop(0, steps, step, 0)

    for half in range(2):
        local(half).wait()
        for j in range(1, peers):
            remote(half, j).wait_send()
            incoming(half, j).wait_recv()


def attend_and_return(queries, limits, history, gain, peers, key_rows):
    rows, width = queries.shape
    kernel = functools.partial(fused_kernel, peers, key_rows)
    return pl.pallas_call(
        kernel,
        out_shape=jax.ShapeDtypeStruct((rows, width), jnp.bfloat16),
        in_specs=[
            pl.BlockSpec(memory_space=pltpu.VMEM),
            pl.BlockSpec(memory_space=pltpu.VMEM),
            pl.BlockSpec(memory_space=pltpu.VMEM),
            pl.BlockSpec(memory_space=pl.ANY),
        ],
        out_specs=pl.BlockSpec(memory_space=pl.ANY),
        scratch_shapes=[
            pltpu.VMEM((2, key_rows, 2 * width), jnp.bfloat16),
            pltpu.SemaphoreType.DMA((2,)),
            pltpu.VMEM((rows // 2, width), jnp.float32),
            pltpu.VMEM((2, rows // 2, width), jnp.bfloat16),
            pltpu.SemaphoreType.DMA((2, peers)),
            pltpu.SemaphoreType.DMA((2, peers)),
            pltpu.SemaphoreType.DMA((2,)),
        ],
        compiler_params=pltpu.CompilerParams(
            collective_id=0, has_side_effects=True, vmem_limit_bytes=60 * 1024 * 1024
        ),
        cost_estimate=pl.CostEstimate(
            flops=8 * rows * history.shape[0] * width,
            transcendentals=rows * history.shape[0] * HEADS,
            bytes_accessed=2 * history.size * 2 + rows * width * 6,
        ),
    )(queries, limits, gain.reshape(1, width), history)


def per_device(cand_x, cand_user, visible, hist_len, kv_cache, w_in, w_out, ln_gain):
    rows, width = cand_x.shape
    columns = lax.axis_size("cand")
    capacity = 2 * rows // columns
    slots = columns * capacity
    hidden = jax.nn.silu(jnp.dot(cand_x, w_in, preferred_element_type=jnp.float32))
    queries = hidden[:, :width].astype(jnp.bfloat16)
    gate = hidden[:, width:].astype(jnp.bfloat16)
    owner = cand_user[:, 0]
    onehot = (owner[:, None] == jnp.arange(columns, dtype=jnp.int32)[None, :]).astype(jnp.int32)
    earlier = jnp.cumsum(onehot, axis=0) - onehot
    slot_of = owner * capacity + jnp.sum(earlier * onehot, axis=1)
    send_rows = jnp.zeros((slots, width), jnp.bfloat16).at[slot_of].set(queries)
    send_vis = jnp.zeros((slots,), jnp.bfloat16).at[slot_of].set(visible.astype(jnp.bfloat16))
    got_rows, got_vis = (
        lax.all_to_all(
            send_rows.reshape(columns, capacity, width),
            "cand",
            split_axis=0,
            concat_axis=0,
            tiled=True,
        ),
        lax.all_to_all(
            send_vis.reshape(columns, capacity), "cand", split_axis=0, concat_axis=0, tiled=True
        ),
    )
    got_rows = got_rows.reshape(slots, width)
    got_vis = got_vis.reshape(slots)
    user_length = hist_len[0].astype(jnp.float32)
    limits = jnp.minimum(user_length, BLK * got_vis.astype(jnp.float32)).astype(jnp.int32)
    halves = lambda x: jnp.swapaxes(x.reshape(columns, 2, capacity // 2, -1), 0, 1).reshape(slots, -1)
    segment = kv_cache[0]
    history = lax.all_gather(segment, "user", axis=0, tiled=True)
    returned = attend_and_return(
        halves(got_rows), halves(limits.reshape(slots, 1)), history, ln_gain, columns, segment.shape[0]
    )
    pick = (slot_of[:, None] == jnp.arange(slots, dtype=jnp.int32)[None, :]).astype(jnp.bfloat16)
    home_rows = jnp.dot(pick, returned, preferred_element_type=jnp.float32)
    mixed_rows = (home_rows.astype(jnp.float32) * gate.astype(jnp.float32)).astype(jnp.bfloat16)
    projected = jnp.dot(mixed_rows, w_out, preferred_element_type=jnp.float32)
    return (cand_x.astype(jnp.float32) + projected).astype(jnp.bfloat16)


def solution(mesh):
    in_specs = (
        P(("user", "cand"), None),
        P(("user", "cand"), None),
        P(("user", "cand")),
        P("cand"),
        P("cand", "user", None),
        P(),
        P(),
        P(),
    )
    out_specs = P(("user", "cand"), None)
    return jax.shard_map(
        per_device, mesh=mesh, in_specs=in_specs, out_specs=out_specs, check_vma=False
    )
```

```python
import functools
import math

import jax
import jax.numpy as jnp
from jax import lax
from jax.experimental import pallas as pl
from jax.experimental.pallas import tpu as pltpu
from jax.sharding import PartitionSpec as P

HEADS = 8
BLK = 128
SUB_ROWS = 1024

norm_eps = 1e-06


def attend_kernel(seg_rows, skip_own, base_ref, q_ref, lim_ref, kv_ref, acc_ref, o_ref):
    k = pl.program_id(0)
    me = base_ref[0]
    width = q_ref.shape[1]
    head_size = width // HEADS
    tk = kv_ref.shape[0]
    rows = q_ref.shape[0]
    half_scale = 0.5 / math.sqrt(head_size)

    @pl.when(k == 0)
    def _():
        o_ref[...] = acc_ref[...]

    if skip_own:
        start = k * seg_rows
        run = k != me
    else:
        start = me * seg_rows + k * tk
        run = k >= 0

    @pl.when(run)
    def _():
        def sub(r, carry):
            r0 = pl.multiple_of(r * SUB_ROWS, SUB_ROWS)
            lim = lim_ref[pl.ds(r0, SUB_ROWS), :]
            pos = start + lax.broadcasted_iota(jnp.int32, (SUB_ROWS, tk), 1)
            vis = pos < lim
            for h in range(HEADS):
                cols = slice(h * head_size, (h + 1) * head_size)
                qh = q_ref[pl.ds(r0, SUB_ROWS), cols]
                kh = kv_ref[:, cols]
                s = lax.dot_general(
                    qh, kh, (((1,), (1,)), ((), ())), preferred_element_type=jnp.float32
                )
                t = s * half_scale
                w = jnp.where(vis, t + t * jnp.tanh(t), 0.0).astype(jnp.bfloat16)
                vh = kv_ref[:, width + h * head_size : width + (h + 1) * head_size]
                o_ref[pl.ds(r0, SUB_ROWS), cols] += jnp.dot(
                    w, vh, preferred_element_type=jnp.float32
                )
            return carry

        lax.fori_loop(0, rows // SUB_ROWS, sub, 0)


def attend(queries, limits, kv, acc, base, seg_rows, skip_own):
    rows, width = queries.shape
    kv_rows = kv.shape[0]
    tk = seg_rows
    steps = kv_rows // tk
    kernel = functools.partial(attend_kernel, seg_rows, skip_own)
    flops = 4 * rows * kv_rows * width
    return pl.pallas_call(
        kernel,
        out_shape=jax.ShapeDtypeStruct((rows, width), jnp.float32),
        grid_spec=pltpu.PrefetchScalarGridSpec(
            num_scalar_prefetch=1,
            grid=(steps,),
            in_specs=[
                pl.BlockSpec((rows, width), lambda k, b: (0, 0)),
                pl.BlockSpec((rows, 1), lambda k, b: (0, 0)),
                pl.BlockSpec((tk, 2 * width), lambda k, b: (k, 0)),
                pl.BlockSpec((rows, width), lambda k, b: (0, 0)),
            ],
            out_specs=pl.BlockSpec((rows, width), lambda k, b: (0, 0)),
        ),
        input_output_aliases={4: 0},
        compiler_params=pltpu.CompilerParams(
            dimension_semantics=("arbitrary",), vmem_limit_bytes=60 * 1024 * 1024
        ),
        cost_estimate=pl.CostEstimate(
            flops=flops,
            transcendentals=rows * kv_rows * HEADS,
            bytes_accessed=kv_rows * 2 * width * 2 + rows * width * 10,
        ),
    )(base, queries, limits, kv, acc)


def fused_kernel(peers, key_rows, q_ref, lim_ref, gain_ref, hist_hbm, start_hbm, out_hbm,
                 kv_buf, kv_sem, acc, normed, send_sem, recv_sem, local_sem, start_sem):
    me = lax.axis_index("cand")
    uid = lax.axis_index("user")
    rows, width = q_ref.shape
    half_rows = rows // 2
    blk = half_rows // peers
    cap = 2 * blk
    head_size = width // HEADS
    half_scale = 0.5 / math.sqrt(head_size)
    segments = hist_hbm.shape[0] // key_rows - 1
    steps = 2 * segments
    own = lax.axis_index("user")

    barrier = pltpu.get_barrier_semaphore()
    for j in range(1, peers):
        pl.semaphore_signal(
            barrier, inc=1, device_id=(uid, lax.rem(me + j, peers)), device_id_type=pl.DeviceIdType.MESH
        )
    pl.semaphore_wait(barrier, peers - 1)

    def start_copy(half):
        return pltpu.make_async_copy(
            start_hbm.at[pl.ds(half * half_rows, half_rows)], acc.at[half], start_sem.at[half]
        )

    def kv_copy(s, slot):
        k = lax.rem(own + 1 + lax.rem(s, segments), segments + 1)
        return pltpu.make_async_copy(
            hist_hbm.at[pl.ds(pl.multiple_of(k * key_rows, key_rows), key_rows)],
            kv_buf.at[slot],
            kv_sem.at[slot],
        )

    def remote(half, j):
        p = lax.rem(me + j, peers)
        return pltpu.make_async_remote_copy(
            src_ref=normed.at[half, pl.ds(pl.multiple_of(p * blk, blk), blk)],
            dst_ref=out_hbm.at[pl.ds(pl.multiple_of(me * cap + half * blk, blk), blk)],
            send_sem=send_sem.at[half, j],
            recv_sem=recv_sem.at[half, j],
            device_id=(uid, p),
            device_id_type=pl.DeviceIdType.MESH,
        )

    def incoming(half, j):
        src = lax.rem(me + peers - j, peers)
        return pltpu.make_async_remote_copy(
            src_ref=normed.at[half, pl.ds(pl.multiple_of(me * blk, blk), blk)],
            dst_ref=out_hbm.at[pl.ds(pl.multiple_of(src * cap + half * blk, blk), blk)],
            send_sem=send_sem.at[half, j],
            recv_sem=recv_sem.at[half, j],
            device_id=(uid, src),
            device_id_type=pl.DeviceIdType.MESH,
        )

    def local(half):
        return pltpu.make_async_copy(
            normed.at[half, pl.ds(pl.multiple_of(me * blk, blk), blk)],
            out_hbm.at[pl.ds(pl.multiple_of(me * cap + half * blk, blk), blk)],
            local_sem.at[half],
        )

    kv_copy(0, 0).start()
    start_copy(0).start()
    start_copy(1).start()

    def step(s, carry):
        slot = lax.rem(s, 2)
        half = s // segments
        i = lax.rem(s, segments)
        k = lax.rem(own + 1 + i, segments + 1)
        kv_copy(s, slot).wait()

        @pl.when(s + 1 < steps)
        def _():
            kv_copy(s + 1, 1 - slot).start()

        @pl.when(s == 0)
        def _():
            start_copy(0).wait()

        @pl.when(s == segments)
        def _():
            start_copy(1).wait()

        total = acc.at[half]
        q_rows = pl.ds(pl.multiple_of(half * half_rows, half_rows), half_rows)
        pos = k * key_rows + lax.broadcasted_iota(jnp.int32, (half_rows, key_rows), 1)
        vis = pos < lim_ref[q_rows, :]
        block = kv_buf.at[slot]
        for h in range(HEADS):
            cols = slice(h * head_size, (h + 1) * head_size)
            scores = lax.dot_general(
                q_ref[q_rows, cols],
                block[:, cols],
                (((1,), (1,)), ((), ())),
                preferred_element_type=jnp.float32,
            )
            t = scores * half_scale
            w = jnp.where(vis, t + t * jnp.tanh(t), 0.0).astype(jnp.bfloat16)
            vh = block[:, width + h * head_size : width + (h + 1) * head_size]
            total[:, cols] += jnp.dot(w, vh, preferred_element_type=jnp.float32)

        @pl.when(i == segments - 1)
        def _():
            value = total[...]
            mean_row = jnp.mean(value, axis=1, keepdims=True)
            centered = value - mean_row
            variance = jnp.mean(centered * centered, axis=1, keepdims=True)
            scale_row = lax.rsqrt(variance + norm_eps)
            normed[half] = (centered * scale_row * gain_ref[...]).astype(jnp.bfloat16)
            local(half).start()
            for j in range(1, peers):
                remote(half, j).start()

        return carry

    lax.fori_loop(0, steps, step, 0)

    for half in range(2):
        local(half).wait()
        for j in range(1, peers):
            remote(half, j).wait_send()
            incoming(half, j).wait_recv()


def attend_and_return(queries, limits, history, start, gain, peers, key_rows):
    rows, width = queries.shape
    kernel = functools.partial(fused_kernel, peers, key_rows)
    return pl.pallas_call(
        kernel,
        out_shape=jax.ShapeDtypeStruct((rows, width), jnp.bfloat16),
        in_specs=[
            pl.BlockSpec(memory_space=pltpu.VMEM),
            pl.BlockSpec(memory_space=pltpu.VMEM),
            pl.BlockSpec(memory_space=pltpu.VMEM),
            pl.BlockSpec(memory_space=pl.ANY),
            pl.BlockSpec(memory_space=pl.ANY),
        ],
        out_specs=pl.BlockSpec(memory_space=pl.ANY),
        scratch_shapes=[
            pltpu.VMEM((2, key_rows, 2 * width), jnp.bfloat16),
            pltpu.SemaphoreType.DMA((2,)),
            pltpu.VMEM((2, rows // 2, width), jnp.float32),
            pltpu.VMEM((2, rows // 2, width), jnp.bfloat16),
            pltpu.SemaphoreType.DMA((2, peers)),
            pltpu.SemaphoreType.DMA((2, peers)),
            pltpu.SemaphoreType.DMA((2,)),
            pltpu.SemaphoreType.DMA((2,)),
        ],
        compiler_params=pltpu.CompilerParams(
            collective_id=0, has_side_effects=True, vmem_limit_bytes=60 * 1024 * 1024
        ),
        cost_estimate=pl.CostEstimate(
            flops=8 * rows * history.shape[0] * width,
            transcendentals=rows * history.shape[0] * HEADS,
            bytes_accessed=2 * history.size * 2 + rows * width * 6,
        ),
    )(queries, limits, gain.reshape(1, width), history, start)


def per_device(cand_x, cand_user, visible, hist_len, kv_cache, w_in, w_out, ln_gain):
    rows, width = cand_x.shape
    columns = lax.axis_size("cand")
    capacity = 2 * rows // columns
    slots = columns * capacity
    hidden = jax.nn.silu(jnp.dot(cand_x, w_in, preferred_element_type=jnp.float32))
    queries = hidden[:, :width].astype(jnp.bfloat16)
    gate = hidden[:, width:].astype(jnp.bfloat16)
    owner = cand_user[:, 0]
    onehot = (owner[:, None] == jnp.arange(columns, dtype=jnp.int32)[None, :]).astype(jnp.int32)
    earlier = jnp.cumsum(onehot, axis=0) - onehot
    slot_of = owner * capacity + jnp.sum(earlier * onehot, axis=1)
    send_rows = jnp.zeros((slots, width), jnp.bfloat16).at[slot_of].set(queries)
    send_vis = jnp.zeros((slots,), jnp.bfloat16).at[slot_of].set(visible.astype(jnp.bfloat16))
    got_rows, got_vis = (
        lax.all_to_all(
            send_rows.reshape(columns, capacity, width),
            "cand",
            split_axis=0,
            concat_axis=0,
            tiled=True,
        ),
        lax.all_to_all(
            send_vis.reshape(columns, capacity), "cand", split_axis=0, concat_axis=0, tiled=True
        ),
    )
    got_rows = got_rows.reshape(slots, width)
    got_vis = got_vis.reshape(slots)
    user_length = hist_len[0].astype(jnp.float32)
    limits = jnp.minimum(user_length, BLK * got_vis.astype(jnp.float32)).astype(jnp.int32)
    halves = lambda x: jnp.swapaxes(x.reshape(columns, 2, capacity // 2, -1), 0, 1).reshape(slots, -1)
    segment = kv_cache[0]
    me = lax.axis_index("user").astype(jnp.int32).reshape(1)
    queries_h = halves(got_rows)
    limits_h = halves(limits.reshape(slots, 1))
    start = attend(
        queries_h, limits_h, segment, jnp.zeros((slots, width), jnp.float32), me, segment.shape[0], False
    )
    history = lax.all_gather(segment, "user", axis=0, tiled=True)
    returned = attend_and_return(
        queries_h, limits_h, history, start, ln_gain, columns, segment.shape[0]
    )
    pick = (slot_of[:, None] == jnp.arange(slots, dtype=jnp.int32)[None, :]).astype(jnp.bfloat16)
    home_rows = jnp.dot(pick, returned, preferred_element_type=jnp.float32)
    mixed_rows = (home_rows.astype(jnp.float32) * gate.astype(jnp.float32)).astype(jnp.bfloat16)
    projected = jnp.dot(mixed_rows, w_out, preferred_element_type=jnp.float32)
    return (cand_x.astype(jnp.float32) + projected).astype(jnp.bfloat16)


def solution(mesh):
    in_specs = (
        P(("user", "cand"), None),
        P(("user", "cand"), None),
        P(("user", "cand")),
        P("cand"),
        P("cand", "user", None),
        P(),
        P(),
        P(),
    )
    out_specs = P(("user", "cand"), None)
    return jax.shard_map(
        per_device, mesh=mesh, in_specs=in_specs, out_specs=out_specs, check_vma=False
    )
```

```python
import functools
import math

import jax
import jax.numpy as jnp
from jax import lax
from jax.experimental import pallas as pl
from jax.experimental.pallas import tpu as pltpu
from jax.sharding import PartitionSpec as P

HEADS = 8
BLK = 128
SUB_ROWS = 1024

norm_eps = 1e-06


def attend_kernel(seg_rows, skip_own, base_ref, q_ref, lim_ref, kv_ref, acc_ref, o_ref):
    k = pl.program_id(0)
    me = base_ref[0]
    width = q_ref.shape[1]
    head_size = width // HEADS
    tk = kv_ref.shape[0]
    rows = q_ref.shape[0]
    half_scale = 0.5 / math.sqrt(head_size)

    @pl.when(k == 0)
    def _():
        o_ref[...] = acc_ref[...]

    if skip_own:
        start = k * seg_rows
        run = k != me
    else:
        start = me * seg_rows + k * tk
        run = k >= 0

    @pl.when(run)
    def _():
        def sub(r, carry):
            r0 = pl.multiple_of(r * SUB_ROWS, SUB_ROWS)
            lim = lim_ref[pl.ds(r0, SUB_ROWS), :]
            pos = start + lax.broadcasted_iota(jnp.int32, (SUB_ROWS, tk), 1)
            vis = pos < lim
            for h in range(HEADS):
                cols = slice(h * head_size, (h + 1) * head_size)
                qh = q_ref[pl.ds(r0, SUB_ROWS), cols]
                kh = kv_ref[:, cols]
                s = lax.dot_general(
                    qh, kh, (((1,), (1,)), ((), ())), preferred_element_type=jnp.float32
                )
                t = s * half_scale
                w = jnp.where(vis, t + t * jnp.tanh(t), 0.0).astype(jnp.bfloat16)
                vh = kv_ref[:, width + h * head_size : width + (h + 1) * head_size]
                o_ref[pl.ds(r0, SUB_ROWS), cols] += jnp.dot(
                    w, vh, preferred_element_type=jnp.float32
                )
            return carry

        lax.fori_loop(0, rows // SUB_ROWS, sub, 0)


def attend(queries, limits, kv, acc, base, seg_rows, skip_own):
    rows, width = queries.shape
    kv_rows = kv.shape[0]
    tk = seg_rows
    steps = kv_rows // tk
    kernel = functools.partial(attend_kernel, seg_rows, skip_own)
    flops = 4 * rows * kv_rows * width
    return pl.pallas_call(
        kernel,
        out_shape=jax.ShapeDtypeStruct((rows, width), jnp.float32),
        grid_spec=pltpu.PrefetchScalarGridSpec(
            num_scalar_prefetch=1,
            grid=(steps,),
            in_specs=[
                pl.BlockSpec((rows, width), lambda k, b: (0, 0)),
                pl.BlockSpec((rows, 1), lambda k, b: (0, 0)),
                pl.BlockSpec((tk, 2 * width), lambda k, b: (k, 0)),
                pl.BlockSpec((rows, width), lambda k, b: (0, 0)),
            ],
            out_specs=pl.BlockSpec((rows, width), lambda k, b: (0, 0)),
        ),
        input_output_aliases={4: 0},
        compiler_params=pltpu.CompilerParams(
            dimension_semantics=("arbitrary",), vmem_limit_bytes=60 * 1024 * 1024
        ),
        cost_estimate=pl.CostEstimate(
            flops=flops,
            transcendentals=rows * kv_rows * HEADS,
            bytes_accessed=kv_rows * 2 * width * 2 + rows * width * 10,
        ),
    )(base, queries, limits, kv, acc)


def fused_kernel(peers, key_rows, parts, q_ref, lim_ref, gain_ref, hist_hbm, start_hbm, out_hbm,
                 kv_buf, kv_sem, acc, normed, send_sem, recv_sem, local_sem, start_sem):
    me = lax.axis_index("cand")
    uid = lax.axis_index("user")
    rows, width = q_ref.shape
    cap = rows // peers
    head_size = width // HEADS
    half_scale = 0.5 / math.sqrt(head_size)
    segments = hist_hbm.shape[0] // key_rows - 1
    steps = len(parts) * segments

    barrier = pltpu.get_barrier_semaphore()
    for j in range(1, peers):
        pl.semaphore_signal(
            barrier, inc=1, device_id=(uid, lax.rem(me + j, peers)), device_id_type=pl.DeviceIdType.MESH
        )
    pl.semaphore_wait(barrier, peers - 1)

    def part_rows(n):
        first, count = parts[n]
        return first * peers, count * peers

    def start_copy(n):
        r0, nr = part_rows(n)
        return pltpu.make_async_copy(
            start_hbm.at[pl.ds(r0, nr)], acc.at[pl.ds(r0, nr)], start_sem.at[n]
        )

    def kv_copy(s, slot):
        k = lax.rem(uid + 1 + lax.rem(s, segments), segments + 1)
        return pltpu.make_async_copy(
            hist_hbm.at[pl.ds(pl.multiple_of(k * key_rows, key_rows), key_rows)],
            kv_buf.at[slot],
            kv_sem.at[slot],
        )

    def remote(n, j, dest, src):
        first, count = parts[n]
        r0 = first * peers
        return pltpu.make_async_remote_copy(
            src_ref=normed.at[pl.ds(r0 + dest * count, count)],
            dst_ref=out_hbm.at[pl.ds(src * cap + first, count)],
            send_sem=send_sem.at[n, j],
            recv_sem=recv_sem.at[n, j],
            device_id=(uid, dest),
            device_id_type=pl.DeviceIdType.MESH,
        )

    def local(n):
        first, count = parts[n]
        return pltpu.make_async_copy(
            normed.at[pl.ds(first * peers + me * count, count)],
            out_hbm.at[pl.ds(me * cap + first, count)],
            local_sem.at[n],
        )

    kv_copy(0, 0).start()
    for n in range(len(parts)):
        start_copy(n).start()

    for n in range(len(parts)):
        r0, nr = part_rows(n)
        start_copy(n).wait()
        lim = lim_ref[r0 : r0 + nr, :]

        def step(i, carry, n=n, r0=r0, nr=nr, lim=lim):
            s = n * segments + i
            slot = lax.rem(s, 2)
            k = lax.rem(uid + 1 + i, segments + 1)
            kv_copy(s, slot).wait()

            @pl.when(s + 1 < steps)
            def _():
                kv_copy(s + 1, 1 - slot).start()

            pos = k * key_rows + lax.broadcasted_iota(jnp.int32, (nr, key_rows), 1)
            vis = pos < lim
            block = kv_buf.at[slot]
            for h in range(HEADS):
                cols = slice(h * head_size, (h + 1) * head_size)
                scores = lax.dot_general(
                    q_ref[r0 : r0 + nr, cols],
                    block[:, cols],
                    (((1,), (1,)), ((), ())),
                    preferred_element_type=jnp.float32,
                )
                t = scores * half_scale
                w = jnp.where(vis, t + t * jnp.tanh(t), 0.0).astype(jnp.bfloat16)
                vh = block[:, width + h * head_size : width + (h + 1) * head_size]
                acc[r0 : r0 + nr, cols] += jnp.dot(w, vh, preferred_element_type=jnp.float32)
            return carry

        lax.fori_loop(0, segments, step, 0)
        value = acc[r0 : r0 + nr, :]
        mean_row = jnp.mean(value, axis=1, keepdims=True)
        centered = value - mean_row
        variance = jnp.mean(centered * centered, axis=1, keepdims=True)
        scale_row = lax.rsqrt(variance + norm_eps)
        normed[r0 : r0 + nr, :] = (centered * scale_row * gain_ref[...]).astype(jnp.bfloat16)
        local(n).start()
        for j in range(1, peers):
            remote(n, j, lax.rem(me + j, peers), me).start()

    for n in range(len(parts)):
        local(n).wait()
        for j in range(1, peers):
            remote(n, j, lax.rem(me + j, peers), me).wait_send()
            remote(n, j, me, lax.rem(me + peers - j, peers)).wait_recv()


PARTS = ((0, 16), (16, 32), (48, 16))


def attend_and_return(queries, limits, history, start, gain, peers, key_rows):
    rows, width = queries.shape
    kernel = functools.partial(fused_kernel, peers, key_rows, PARTS)
    return pl.pallas_call(
        kernel,
        out_shape=jax.ShapeDtypeStruct((rows, width), jnp.bfloat16),
        in_specs=[
            pl.BlockSpec(memory_space=pltpu.VMEM),
            pl.BlockSpec(memory_space=pltpu.VMEM),
            pl.BlockSpec(memory_space=pltpu.VMEM),
            pl.BlockSpec(memory_space=pl.ANY),
            pl.BlockSpec(memory_space=pl.ANY),
        ],
        out_specs=pl.BlockSpec(memory_space=pl.ANY),
        scratch_shapes=[
            pltpu.VMEM((2, key_rows, 2 * width), jnp.bfloat16),
            pltpu.SemaphoreType.DMA((2,)),
            pltpu.VMEM((rows, width), jnp.float32),
            pltpu.VMEM((rows, width), jnp.bfloat16),
            pltpu.SemaphoreType.DMA((len(PARTS), peers)),
            pltpu.SemaphoreType.DMA((len(PARTS), peers)),
            pltpu.SemaphoreType.DMA((len(PARTS),)),
            pltpu.SemaphoreType.DMA((len(PARTS),)),
        ],
        compiler_params=pltpu.CompilerParams(
            collective_id=0, has_side_effects=True, vmem_limit_bytes=60 * 1024 * 1024
        ),
        cost_estimate=pl.CostEstimate(
            flops=8 * rows * history.shape[0] * width,
            transcendentals=rows * history.shape[0] * HEADS,
            bytes_accessed=2 * history.size * 2 + rows * width * 6,
        ),
    )(queries, limits, gain.reshape(1, width), history, start)


def per_device(cand_x, cand_user, visible, hist_len, kv_cache, w_in, w_out, ln_gain):
    rows, width = cand_x.shape
    columns = lax.axis_size("cand")
    capacity = 2 * rows // columns
    slots = columns * capacity
    hidden = jax.nn.silu(jnp.dot(cand_x, w_in, preferred_element_type=jnp.float32))
    queries = hidden[:, :width].astype(jnp.bfloat16)
    gate = hidden[:, width:].astype(jnp.bfloat16)
    owner = cand_user[:, 0]
    onehot = (owner[:, None] == jnp.arange(columns, dtype=jnp.int32)[None, :]).astype(jnp.int32)
    earlier = jnp.cumsum(onehot, axis=0) - onehot
    slot_of = owner * capacity + jnp.sum(earlier * onehot, axis=1)
    send_rows = jnp.zeros((slots, width), jnp.bfloat16).at[slot_of].set(queries)
    send_vis = jnp.zeros((slots,), jnp.bfloat16).at[slot_of].set(visible.astype(jnp.bfloat16))
    got_rows, got_vis = (
        lax.all_to_all(
            send_rows.reshape(columns, capacity, width),
            "cand",
            split_axis=0,
            concat_axis=0,
            tiled=True,
        ),
        lax.all_to_all(
            send_vis.reshape(columns, capacity), "cand", split_axis=0, concat_axis=0, tiled=True
        ),
    )
    got_rows = got_rows.reshape(slots, width)
    got_vis = got_vis.reshape(slots)
    user_length = hist_len[0].astype(jnp.float32)
    limits = jnp.minimum(user_length, BLK * got_vis.astype(jnp.float32)).astype(jnp.int32)
    def halves(x):
        x = x.reshape(columns, capacity, -1)
        pieces = [x[:, first : first + count].reshape(-1, x.shape[-1]) for first, count in PARTS]
        return jnp.concatenate(pieces, axis=0)

    segment = kv_cache[0]
    me = lax.axis_index("user").astype(jnp.int32).reshape(1)
    queries_h = halves(got_rows)
    limits_h = halves(limits.reshape(slots, 1))
    start = attend(
        queries_h, limits_h, segment, jnp.zeros((slots, width), jnp.float32), me, segment.shape[0], False
    )
    history = lax.all_gather(segment, "user", axis=0, tiled=True)
    returned = attend_and_return(
        queries_h, limits_h, history, start, ln_gain, columns, segment.shape[0]
    )
    pick = (slot_of[:, None] == jnp.arange(slots, dtype=jnp.int32)[None, :]).astype(jnp.bfloat16)
    home_rows = jnp.dot(pick, returned, preferred_element_type=jnp.float32)
    mixed_rows = (home_rows.astype(jnp.float32) * gate.astype(jnp.float32)).astype(jnp.bfloat16)
    projected = jnp.dot(mixed_rows, w_out, preferred_element_type=jnp.float32)
    return (cand_x.astype(jnp.float32) + projected).astype(jnp.bfloat16)


def solution(mesh):
    in_specs = (
        P(("user", "cand"), None),
        P(("user", "cand"), None),
        P(("user", "cand")),
        P("cand"),
        P("cand", "user", None),
        P(),
        P(),
        P(),
    )
    out_specs = P(("user", "cand"), None)
    return jax.shard_map(
        per_device, mesh=mesh, in_specs=in_specs, out_specs=out_specs, check_vma=False
    )
```

```python
import functools
import math

import jax
import jax.numpy as jnp
from jax import lax
from jax.experimental import pallas as pl
from jax.experimental.pallas import tpu as pltpu
from jax.sharding import PartitionSpec as P

HEADS = 8
BLK = 128
SUB_ROWS = 1024

norm_eps = 1e-06


def attend_kernel(seg_rows, skip_own, base_ref, q_ref, lim_ref, kv_ref, acc_ref, o_ref):
    k = pl.program_id(0)
    me = base_ref[0]
    width = q_ref.shape[1]
    head_size = width // HEADS
    tk = kv_ref.shape[0]
    rows = q_ref.shape[0]
    half_scale = 0.5 / math.sqrt(head_size)

    @pl.when(k == 0)
    def _():
        o_ref[...] = acc_ref[...]

    if skip_own:
        start = k * seg_rows
        run = k != me
    else:
        start = me * seg_rows + k * tk
        run = k >= 0

    @pl.when(run)
    def _():
        def sub(r, carry):
            r0 = pl.multiple_of(r * SUB_ROWS, SUB_ROWS)
            lim = lim_ref[pl.ds(r0, SUB_ROWS), :]
            pos = start + lax.broadcasted_iota(jnp.int32, (SUB_ROWS, tk), 1)
            vis = pos < lim
            for h in range(HEADS):
                cols = slice(h * head_size, (h + 1) * head_size)
                qh = q_ref[pl.ds(r0, SUB_ROWS), cols]
                kh = kv_ref[:, cols]
                s = lax.dot_general(
                    qh, kh, (((1,), (1,)), ((), ())), preferred_element_type=jnp.float32
                )
                t = s * half_scale
                w = jnp.where(vis, t + t * jnp.tanh(t), 0.0).astype(jnp.bfloat16)
                vh = kv_ref[:, width + h * head_size : width + (h + 1) * head_size]
                o_ref[pl.ds(r0, SUB_ROWS), cols] += jnp.dot(
                    w, vh, preferred_element_type=jnp.float32
                )
            return carry

        lax.fori_loop(0, rows // SUB_ROWS, sub, 0)


def attend(queries, limits, kv, acc, base, seg_rows, skip_own):
    rows, width = queries.shape
    kv_rows = kv.shape[0]
    tk = seg_rows
    steps = kv_rows // tk
    kernel = functools.partial(attend_kernel, seg_rows, skip_own)
    flops = 4 * rows * kv_rows * width
    return pl.pallas_call(
        kernel,
        out_shape=jax.ShapeDtypeStruct((rows, width), jnp.float32),
        grid_spec=pltpu.PrefetchScalarGridSpec(
            num_scalar_prefetch=1,
            grid=(steps,),
            in_specs=[
                pl.BlockSpec((rows, width), lambda k, b: (0, 0)),
                pl.BlockSpec((rows, 1), lambda k, b: (0, 0)),
                pl.BlockSpec((tk, 2 * width), lambda k, b: (k, 0)),
                pl.BlockSpec((rows, width), lambda k, b: (0, 0)),
            ],
            out_specs=pl.BlockSpec((rows, width), lambda k, b: (0, 0)),
        ),
        input_output_aliases={4: 0},
        compiler_params=pltpu.CompilerParams(
            dimension_semantics=("arbitrary",), vmem_limit_bytes=60 * 1024 * 1024
        ),
        cost_estimate=pl.CostEstimate(
            flops=flops,
            transcendentals=rows * kv_rows * HEADS,
            bytes_accessed=kv_rows * 2 * width * 2 + rows * width * 10,
        ),
    )(base, queries, limits, kv, acc)


ORDER = (None, (0,1,0),(1,0,0),(1,1,0),(3,0,0),(3,1,0),(2,0,0),(2,1,0),(0,1,1),(1,0,1),(1,1,1),(3,0,1),(3,1,1),(2,0,1),(2,1,1),(0,0,1))


def fused_kernel(peers, key_rows, q_ref, lim_ref, gain_ref, hist_hbm, start_hbm, out_hbm,
                 kv_buf, kv_sem, acc, normed, send_sem, recv_sem, local_sem, start_sem):
    me = lax.axis_index("cand")
    uid = lax.axis_index("user")
    rows, width = q_ref.shape
    half_rows = rows // 2
    blk = half_rows // peers
    cap = 2 * blk
    head_size = width // HEADS
    half_scale = 0.5 / math.sqrt(head_size)
    segments = hist_hbm.shape[0] // key_rows - 1
    steps = 2 * segments
    own = lax.axis_index("user")

    barrier = pltpu.get_barrier_semaphore()
    for j in range(1, peers):
        pl.semaphore_signal(
            barrier, inc=1, device_id=(uid, lax.rem(me + j, peers)), device_id_type=pl.DeviceIdType.MESH
        )
    pl.semaphore_wait(barrier, peers - 1)

    def start_copy(half):
        return pltpu.make_async_copy(
            start_hbm.at[pl.ds(half * half_rows, half_rows)], acc.at[half], start_sem.at[half]
        )

    def kv_copy(s, slot):
        k = lax.rem(own + 1 + lax.rem(s, segments), segments + 1)
        return pltpu.make_async_copy(
            hist_hbm.at[pl.ds(pl.multiple_of(k * key_rows, key_rows), key_rows)],
            kv_buf.at[slot],
            kv_sem.at[slot],
        )

    def peer(j, sign):
        dx, dy, dc = ORDER[j]
        core = lax.rem(me, 2)
        y_lo = lax.rem(me // 2, 2)
        x = me // 4
        return (
            lax.rem(x + sign * dx + 4, 4) * 4
            + lax.rem(y_lo + sign * dy + 2, 2) * 2
            + lax.rem(core + sign * dc + 2, 2)
        )

    def remote(half, j):
        p = peer(j, 1)
        return pltpu.make_async_remote_copy(
            src_ref=normed.at[half, pl.ds(pl.multiple_of(p * blk, blk), blk)],
            dst_ref=out_hbm.at[pl.ds(pl.multiple_of(me * cap + half * blk, blk), blk)],
            send_sem=send_sem.at[half, j],
            recv_sem=recv_sem.at[half, j],
            device_id=(uid, p),
            device_id_type=pl.DeviceIdType.MESH,
        )

    def incoming(half, j):
        src = peer(j, -1)
        return pltpu.make_async_remote_copy(
            src_ref=normed.at[half, pl.ds(pl.multiple_of(me * blk, blk), blk)],
            dst_ref=out_hbm.at[pl.ds(pl.multiple_of(src * cap + half * blk, blk), blk)],
            send_sem=send_sem.at[half, j],
            recv_sem=recv_sem.at[half, j],
            device_id=(uid, src),
            device_id_type=pl.DeviceIdType.MESH,
        )

    def local(half):
        return pltpu.make_async_copy(
            normed.at[half, pl.ds(pl.multiple_of(me * blk, blk), blk)],
            out_hbm.at[pl.ds(pl.multiple_of(me * cap + half * blk, blk), blk)],
            local_sem.at[half],
        )

    kv_copy(0, 0).start()
    start_copy(0).start()
    start_copy(1).start()

    def step(s, carry):
        slot = lax.rem(s, 2)
        half = s // segments
        i = lax.rem(s, segments)
        k = lax.rem(own + 1 + i, segments + 1)
        kv_copy(s, slot).wait()

        @pl.when(s + 1 < steps)
        def _():
            kv_copy(s + 1, 1 - slot).start()

        @pl.when(s == 0)
        def _():
            start_copy(0).wait()

        @pl.when(s == segments)
        def _():
            start_copy(1).wait()

        total = acc.at[half]
        q_rows = pl.ds(pl.multiple_of(half * half_rows, half_rows), half_rows)
        pos = k * key_rows + lax.broadcasted_iota(jnp.int32, (half_rows, key_rows), 1)
        vis = pos < lim_ref[q_rows, :]
        block = kv_buf.at[slot]
        for h in range(HEADS):
            cols = slice(h * head_size, (h + 1) * head_size)
            scores = lax.dot_general(
                q_ref[q_rows, cols],
                block[:, cols],
                (((1,), (1,)), ((), ())),
                preferred_element_type=jnp.float32,
            )
            t = scores * half_scale
            w = jnp.where(vis, t + t * jnp.tanh(t), 0.0).astype(jnp.bfloat16)
            vh = block[:, width + h * head_size : width + (h + 1) * head_size]
            total[:, cols] += jnp.dot(w, vh, preferred_element_type=jnp.float32)

        @pl.when(i == segments - 1)
        def _():
            value = total[...]
            mean_row = jnp.mean(value, axis=1, keepdims=True)
            centered = value - mean_row
            variance = jnp.mean(centered * centered, axis=1, keepdims=True)
            scale_row = lax.rsqrt(variance + norm_eps)
            normed[half] = (centered * scale_row * gain_ref[...]).astype(jnp.bfloat16)
            local(half).start()
            for j in range(1, peers):
                remote(half, j).start()

        return carry

    lax.fori_loop(0, steps, step, 0)

    for half in range(2):
        local(half).wait()
        for j in range(1, peers):
            remote(half, j).wait_send()
            incoming(half, j).wait_recv()


def attend_and_return(queries, limits, history, start, gain, peers, key_rows):
    rows, width = queries.shape
    kernel = functools.partial(fused_kernel, peers, key_rows)
    return pl.pallas_call(
        kernel,
        out_shape=jax.ShapeDtypeStruct((rows, width), jnp.bfloat16),
        in_specs=[
            pl.BlockSpec(memory_space=pltpu.VMEM),
            pl.BlockSpec(memory_space=pltpu.VMEM),
            pl.BlockSpec(memory_space=pltpu.VMEM),
            pl.BlockSpec(memory_space=pl.ANY),
            pl.BlockSpec(memory_space=pl.ANY),
        ],
        out_specs=pl.BlockSpec(memory_space=pl.ANY),
        scratch_shapes=[
            pltpu.VMEM((2, key_rows, 2 * width), jnp.bfloat16),
            pltpu.SemaphoreType.DMA((2,)),
            pltpu.VMEM((2, rows // 2, width), jnp.float32),
            pltpu.VMEM((2, rows // 2, width), jnp.bfloat16),
            pltpu.SemaphoreType.DMA((2, peers)),
            pltpu.SemaphoreType.DMA((2, peers)),
            pltpu.SemaphoreType.DMA((2,)),
            pltpu.SemaphoreType.DMA((2,)),
        ],
        compiler_params=pltpu.CompilerParams(
            collective_id=0, has_side_effects=True, vmem_limit_bytes=60 * 1024 * 1024
        ),
        cost_estimate=pl.CostEstimate(
            flops=8 * rows * history.shape[0] * width,
            transcendentals=rows * history.shape[0] * HEADS,
            bytes_accessed=2 * history.size * 2 + rows * width * 6,
        ),
    )(queries, limits, gain.reshape(1, width), history, start)


def per_device(cand_x, cand_user, visible, hist_len, kv_cache, w_in, w_out, ln_gain):
    rows, width = cand_x.shape
    columns = lax.axis_size("cand")
    capacity = 2 * rows // columns
    slots = columns * capacity
    hidden = jax.nn.silu(jnp.dot(cand_x, w_in, preferred_element_type=jnp.float32))
    queries = hidden[:, :width].astype(jnp.bfloat16)
    gate = hidden[:, width:].astype(jnp.bfloat16)
    owner = cand_user[:, 0]
    onehot = (owner[:, None] == jnp.arange(columns, dtype=jnp.int32)[None, :]).astype(jnp.int32)
    earlier = jnp.cumsum(onehot, axis=0) - onehot
    slot_of = owner * capacity + jnp.sum(earlier * onehot, axis=1)
    send_rows = jnp.zeros((slots, width), jnp.bfloat16).at[slot_of].set(queries)
    send_vis = jnp.zeros((slots,), jnp.bfloat16).at[slot_of].set(visible.astype(jnp.bfloat16))
    got_rows, got_vis = (
        lax.all_to_all(
            send_rows.reshape(columns, capacity, width),
            "cand",
            split_axis=0,
            concat_axis=0,
            tiled=True,
        ),
        lax.all_to_all(
            send_vis.reshape(columns, capacity), "cand", split_axis=0, concat_axis=0, tiled=True
        ),
    )
    got_rows = got_rows.reshape(slots, width)
    got_vis = got_vis.reshape(slots)
    user_length = hist_len[0].astype(jnp.float32)
    limits = jnp.minimum(user_length, BLK * got_vis.astype(jnp.float32)).astype(jnp.int32)
    halves = lambda x: jnp.swapaxes(x.reshape(columns, 2, capacity // 2, -1), 0, 1).reshape(slots, -1)
    segment = kv_cache[0]
    me = lax.axis_index("user").astype(jnp.int32).reshape(1)
    queries_h = halves(got_rows)
    limits_h = halves(limits.reshape(slots, 1))
    start = attend(
        queries_h, limits_h, segment, jnp.zeros((slots, width), jnp.float32), me, segment.shape[0], False
    )
    history = lax.all_gather(segment, "user", axis=0, tiled=True)
    returned = attend_and_return(
        queries_h, limits_h, history, start, ln_gain, columns, segment.shape[0]
    )
    pick = (slot_of[:, None] == jnp.arange(slots, dtype=jnp.int32)[None, :]).astype(jnp.bfloat16)
    home_rows = jnp.dot(pick, returned, preferred_element_type=jnp.float32)
    mixed_rows = (home_rows.astype(jnp.float32) * gate.astype(jnp.float32)).astype(jnp.bfloat16)
    projected = jnp.dot(mixed_rows, w_out, preferred_element_type=jnp.float32)
    return (cand_x.astype(jnp.float32) + projected).astype(jnp.bfloat16)


def solution(mesh):
    in_specs = (
        P(("user", "cand"), None),
        P(("user", "cand"), None),
        P(("user", "cand")),
        P("cand"),
        P("cand", "user", None),
        P(),
        P(),
        P(),
    )
    out_specs = P(("user", "cand"), None)
    return jax.shard_map(
        per_device, mesh=mesh, in_specs=in_specs, out_specs=out_specs, check_vma=False
    )
```

```python
import functools
import math

import jax
import jax.numpy as jnp
from jax import lax
from jax.experimental import pallas as pl
from jax.experimental.pallas import tpu as pltpu
from jax.sharding import PartitionSpec as P

HEADS = 8
BLK = 128
SUB_ROWS = 1024

norm_eps = 1e-06


def attend_kernel(seg_rows, skip_own, base_ref, q_ref, lim_ref, kv_ref, acc_ref, o_ref):
    k = pl.program_id(0)
    me = base_ref[0]
    width = q_ref.shape[1]
    head_size = width // HEADS
    tk = kv_ref.shape[0]
    rows = q_ref.shape[0]
    half_scale = 0.5 / math.sqrt(head_size)

    @pl.when(k == 0)
    def _():
        o_ref[...] = acc_ref[...]

    if skip_own:
        start = k * seg_rows
        run = k != me
    else:
        start = me * seg_rows + k * tk
        run = k >= 0

    @pl.when(run)
    def _():
        def sub(r, carry):
            r0 = pl.multiple_of(r * SUB_ROWS, SUB_ROWS)
            lim = lim_ref[pl.ds(r0, SUB_ROWS), :]
            pos = start + lax.broadcasted_iota(jnp.int32, (SUB_ROWS, tk), 1)
            vis = pos < lim
            for h in range(HEADS):
                cols = slice(h * head_size, (h + 1) * head_size)
                qh = q_ref[pl.ds(r0, SUB_ROWS), cols]
                kh = kv_ref[:, cols]
                s = lax.dot_general(
                    qh, kh, (((1,), (1,)), ((), ())), preferred_element_type=jnp.float32
                )
                t = s * half_scale
                w = jnp.where(vis, t + t * jnp.tanh(t), 0.0).astype(jnp.bfloat16)
                vh = kv_ref[:, width + h * head_size : width + (h + 1) * head_size]
                o_ref[pl.ds(r0, SUB_ROWS), cols] += jnp.dot(
                    w, vh, preferred_element_type=jnp.float32
                )
            return carry

        lax.fori_loop(0, rows // SUB_ROWS, sub, 0)


def attend(queries, limits, kv, acc, base, seg_rows, skip_own):
    rows, width = queries.shape
    kv_rows = kv.shape[0]
    tk = seg_rows
    steps = kv_rows // tk
    kernel = functools.partial(attend_kernel, seg_rows, skip_own)
    flops = 4 * rows * kv_rows * width
    return pl.pallas_call(
        kernel,
        out_shape=jax.ShapeDtypeStruct((rows, width), jnp.float32),
        grid_spec=pltpu.PrefetchScalarGridSpec(
            num_scalar_prefetch=1,
            grid=(steps,),
            in_specs=[
                pl.BlockSpec((rows, width), lambda k, b: (0, 0)),
                pl.BlockSpec((rows, 1), lambda k, b: (0, 0)),
                pl.BlockSpec((tk, 2 * width), lambda k, b: (k, 0)),
                pl.BlockSpec((rows, width), lambda k, b: (0, 0)),
            ],
            out_specs=pl.BlockSpec((rows, width), lambda k, b: (0, 0)),
        ),
        input_output_aliases={4: 0},
        compiler_params=pltpu.CompilerParams(
            dimension_semantics=("arbitrary",), vmem_limit_bytes=60 * 1024 * 1024
        ),
        cost_estimate=pl.CostEstimate(
            flops=flops,
            transcendentals=rows * kv_rows * HEADS,
            bytes_accessed=kv_rows * 2 * width * 2 + rows * width * 10,
        ),
    )(base, queries, limits, kv, acc)


ORDER = (None, (0,1,0),(1,0,0),(1,1,0),(3,0,0),(3,1,0),(2,0,0),(2,1,0),(0,1,1),(1,0,1),(1,1,1),(3,0,1),(3,1,1),(2,0,1),(2,1,1),(0,0,1))


def fused_kernel(peers, key_rows, q_ref, lim_ref, gain_ref, hist_hbm, start_hbm, out_hbm,
                 kv_buf, kv_sem, acc, normed, send_sem, recv_sem, local_sem, start_sem):
    me = lax.axis_index("cand")
    uid = lax.axis_index("user")
    rows, width = q_ref.shape
    half_rows = rows // 2
    blk = half_rows // peers
    cap = 2 * blk
    head_size = width // HEADS
    half_scale = 0.5 / math.sqrt(head_size)
    segments = hist_hbm.shape[0] // key_rows - 1
    steps = 2 * segments
    own = lax.axis_index("user")

    barrier = pltpu.get_barrier_semaphore()
    for j in range(1, peers):
        pl.semaphore_signal(
            barrier, inc=1, device_id=(uid, lax.rem(me + j, peers)), device_id_type=pl.DeviceIdType.MESH
        )

    def start_copy(half):
        return pltpu.make_async_copy(
            start_hbm.at[pl.ds(half * half_rows, half_rows)], acc.at[half], start_sem.at[half]
        )

    def kv_copy(s, slot):
        k = lax.rem(own + 1 + lax.rem(s, segments), segments + 1)
        return pltpu.make_async_copy(
            hist_hbm.at[pl.ds(pl.multiple_of(k * key_rows, key_rows), key_rows)],
            kv_buf.at[slot],
            kv_sem.at[slot],
        )

    def peer(j, sign):
        dx, dy, dc = ORDER[j]
        core = lax.rem(me, 2)
        y_lo = lax.rem(me // 2, 2)
        x = me // 4
        return (
            lax.rem(x + sign * dx + 4, 4) * 4
            + lax.rem(y_lo + sign * dy + 2, 2) * 2
            + lax.rem(core + sign * dc + 2, 2)
        )

    def remote(half, j):
        p = peer(j, 1)
        return pltpu.make_async_remote_copy(
            src_ref=normed.at[half, pl.ds(pl.multiple_of(p * blk, blk), blk)],
            dst_ref=out_hbm.at[pl.ds(pl.multiple_of(me * cap + half * blk, blk), blk)],
            send_sem=send_sem.at[half, j],
            recv_sem=recv_sem.at[half, j],
            device_id=(uid, p),
            device_id_type=pl.DeviceIdType.MESH,
        )

    def incoming(half, j):
        src = peer(j, -1)
        return pltpu.make_async_remote_copy(
            src_ref=normed.at[half, pl.ds(pl.multiple_of(me * blk, blk), blk)],
            dst_ref=out_hbm.at[pl.ds(pl.multiple_of(src * cap + half * blk, blk), blk)],
            send_sem=send_sem.at[half, j],
            recv_sem=recv_sem.at[half, j],
            device_id=(uid, src),
            device_id_type=pl.DeviceIdType.MESH,
        )

    def local(half):
        return pltpu.make_async_copy(
            normed.at[half, pl.ds(pl.multiple_of(me * blk, blk), blk)],
            out_hbm.at[pl.ds(pl.multiple_of(me * cap + half * blk, blk), blk)],
            local_sem.at[half],
        )

    kv_copy(0, 0).start()
    start_copy(0).start()
    start_copy(1).start()

    for half in range(2):
        start_copy(half).wait()
        total = acc.at[half]

        def step(i, carry, half=half, total=total):
            s = half * segments + i
            slot = lax.rem(s, 2)
            k = lax.rem(own + 1 + i, segments + 1)
            kv_copy(s, slot).wait()

            @pl.when(s + 1 < steps)
            def _():
                kv_copy(s + 1, 1 - slot).start()

            q_rows = pl.ds(half * half_rows, half_rows)
            pos = k * key_rows + lax.broadcasted_iota(jnp.int32, (half_rows, key_rows), 1)
            vis = pos < lim_ref[q_rows, :]
            block = kv_buf.at[slot]
            for h in range(HEADS):
                cols = slice(h * head_size, (h + 1) * head_size)
                scores = lax.dot_general(
                    q_ref[q_rows, cols],
                    block[:, cols],
                    (((1,), (1,)), ((), ())),
                    preferred_element_type=jnp.float32,
                )
                t = scores * half_scale
                w = jnp.where(vis, t + t * jnp.tanh(t), 0.0).astype(jnp.bfloat16)
                vh = block[:, width + h * head_size : width + (h + 1) * head_size]
                total[:, cols] += jnp.dot(w, vh, preferred_element_type=jnp.float32)
            return carry

        lax.fori_loop(0, segments, step, 0)
        value = total[...]
        mean_row = jnp.mean(value, axis=1, keepdims=True)
        centered = value - mean_row
        variance = jnp.mean(centered * centered, axis=1, keepdims=True)
        scale_row = lax.rsqrt(variance + norm_eps)
        normed[half] = (centered * scale_row * gain_ref[...]).astype(jnp.bfloat16)
        if half == 0:
            pl.semaphore_wait(barrier, peers - 1)
        local(half).start()
        for j in range(1, peers):
            remote(half, j).start()


    for half in range(2):
        local(half).wait()
        for j in range(1, peers):
            remote(half, j).wait_send()
            incoming(half, j).wait_recv()


def attend_and_return(queries, limits, history, start, gain, peers, key_rows):
    rows, width = queries.shape
    kernel = functools.partial(fused_kernel, peers, key_rows)
    return pl.pallas_call(
        kernel,
        out_shape=jax.ShapeDtypeStruct((rows, width), jnp.bfloat16),
        in_specs=[
            pl.BlockSpec(memory_space=pltpu.VMEM),
            pl.BlockSpec(memory_space=pltpu.VMEM),
            pl.BlockSpec(memory_space=pltpu.VMEM),
            pl.BlockSpec(memory_space=pl.ANY),
            pl.BlockSpec(memory_space=pl.ANY),
        ],
        out_specs=pl.BlockSpec(memory_space=pl.ANY),
        scratch_shapes=[
            pltpu.VMEM((2, key_rows, 2 * width), jnp.bfloat16),
            pltpu.SemaphoreType.DMA((2,)),
            pltpu.VMEM((2, rows // 2, width), jnp.float32),
            pltpu.VMEM((2, rows // 2, width), jnp.bfloat16),
            pltpu.SemaphoreType.DMA((2, peers)),
            pltpu.SemaphoreType.DMA((2, peers)),
            pltpu.SemaphoreType.DMA((2,)),
            pltpu.SemaphoreType.DMA((2,)),
        ],
        compiler_params=pltpu.CompilerParams(
            collective_id=0, has_side_effects=True, vmem_limit_bytes=60 * 1024 * 1024
        ),
        cost_estimate=pl.CostEstimate(
            flops=8 * rows * history.shape[0] * width,
            transcendentals=rows * history.shape[0] * HEADS,
            bytes_accessed=2 * history.size * 2 + rows * width * 6,
        ),
    )(queries, limits, gain.reshape(1, width), history, start)


def per_device(cand_x, cand_user, visible, hist_len, kv_cache, w_in, w_out, ln_gain):
    rows, width = cand_x.shape
    columns = lax.axis_size("cand")
    capacity = 2 * rows // columns
    slots = columns * capacity
    hidden = jax.nn.silu(jnp.dot(cand_x, w_in, preferred_element_type=jnp.float32))
    queries = hidden[:, :width].astype(jnp.bfloat16)
    gate = hidden[:, width:].astype(jnp.bfloat16)
    owner = cand_user[:, 0]
    onehot = (owner[:, None] == jnp.arange(columns, dtype=jnp.int32)[None, :]).astype(jnp.int32)
    earlier = jnp.cumsum(onehot, axis=0) - onehot
    slot_of = owner * capacity + jnp.sum(earlier * onehot, axis=1)
    send_rows = jnp.zeros((slots, width), jnp.bfloat16).at[slot_of].set(queries)
    send_vis = jnp.zeros((slots,), jnp.bfloat16).at[slot_of].set(visible.astype(jnp.bfloat16))
    got_rows, got_vis = (
        lax.all_to_all(
            send_rows.reshape(columns, capacity, width),
            "cand",
            split_axis=0,
            concat_axis=0,
            tiled=True,
        ),
        lax.all_to_all(
            send_vis.reshape(columns, capacity), "cand", split_axis=0, concat_axis=0, tiled=True
        ),
    )
    got_rows = got_rows.reshape(slots, width)
    got_vis = got_vis.reshape(slots)
    user_length = hist_len[0].astype(jnp.float32)
    limits = jnp.minimum(user_length, BLK * got_vis.astype(jnp.float32)).astype(jnp.int32)
    halves = lambda x: jnp.swapaxes(x.reshape(columns, 2, capacity // 2, -1), 0, 1).reshape(slots, -1)
    segment = kv_cache[0]
    me = lax.axis_index("user").astype(jnp.int32).reshape(1)
    queries_h = halves(got_rows)
    limits_h = halves(limits.reshape(slots, 1))
    start = attend(
        queries_h, limits_h, segment, jnp.zeros((slots, width), jnp.float32), me, segment.shape[0], False
    )
    history = lax.all_gather(segment, "user", axis=0, tiled=True)
    returned = attend_and_return(
        queries_h, limits_h, history, start, ln_gain, columns, segment.shape[0]
    )
    pick = (slot_of[:, None] == jnp.arange(slots, dtype=jnp.int32)[None, :]).astype(jnp.bfloat16)
    home_rows = jnp.dot(pick, returned, preferred_element_type=jnp.float32)
    mixed_rows = (home_rows.astype(jnp.float32) * gate.astype(jnp.float32)).astype(jnp.bfloat16)
    projected = jnp.dot(mixed_rows, w_out, preferred_element_type=jnp.float32)
    return (cand_x.astype(jnp.float32) + projected).astype(jnp.bfloat16)


def solution(mesh):
    in_specs = (
        P(("user", "cand"), None),
        P(("user", "cand"), None),
        P(("user", "cand")),
        P("cand"),
        P("cand", "user", None),
        P(),
        P(),
        P(),
    )
    out_specs = P(("user", "cand"), None)
    return jax.shard_map(
        per_device, mesh=mesh, in_specs=in_specs, out_specs=out_specs, check_vma=False
    )
```

```python
import functools
import math

import jax
import jax.numpy as jnp
from jax import lax
from jax.experimental import pallas as pl
from jax.experimental.pallas import tpu as pltpu
from jax.sharding import PartitionSpec as P

HEADS = 8
BLK = 128
SUB_ROWS = 1024

norm_eps = 1e-06


def attend_kernel(seg_rows, skip_own, base_ref, q_ref, lim_ref, kv_ref, acc_ref, o_ref):
    k = pl.program_id(0)
    me = base_ref[0]
    width = q_ref.shape[1]
    head_size = width // HEADS
    tk = kv_ref.shape[0]
    rows = q_ref.shape[0]
    half_scale = 0.5 / math.sqrt(head_size)

    @pl.when(k == 0)
    def _():
        o_ref[...] = acc_ref[...]

    if skip_own:
        start = k * seg_rows
        run = k != me
    else:
        start = me * seg_rows + k * tk
        run = k >= 0

    @pl.when(run)
    def _():
        def sub(r, carry):
            r0 = pl.multiple_of(r * SUB_ROWS, SUB_ROWS)
            lim = lim_ref[pl.ds(r0, SUB_ROWS), :]
            pos = start + lax.broadcasted_iota(jnp.int32, (SUB_ROWS, tk), 1)
            vis = pos < lim
            for h in range(HEADS):
                cols = slice(h * head_size, (h + 1) * head_size)
                qh = q_ref[pl.ds(r0, SUB_ROWS), cols]
                kh = kv_ref[:, cols]
                s = lax.dot_general(
                    qh, kh, (((1,), (1,)), ((), ())), preferred_element_type=jnp.float32
                )
                t = s * half_scale
                w = jnp.where(vis, t + t * jnp.tanh(t), 0.0).astype(jnp.bfloat16)
                vh = kv_ref[:, width + h * head_size : width + (h + 1) * head_size]
                o_ref[pl.ds(r0, SUB_ROWS), cols] += jnp.dot(
                    w, vh, preferred_element_type=jnp.float32
                )
            return carry

        lax.fori_loop(0, rows // SUB_ROWS, sub, 0)


def attend(queries, limits, kv, acc, base, seg_rows, skip_own):
    rows, width = queries.shape
    kv_rows = kv.shape[0]
    tk = seg_rows
    steps = kv_rows // tk
    kernel = functools.partial(attend_kernel, seg_rows, skip_own)
    flops = 4 * rows * kv_rows * width
    return pl.pallas_call(
        kernel,
        out_shape=jax.ShapeDtypeStruct((rows, width), jnp.float32),
        grid_spec=pltpu.PrefetchScalarGridSpec(
            num_scalar_prefetch=1,
            grid=(steps,),
            in_specs=[
                pl.BlockSpec((rows, width), lambda k, b: (0, 0)),
                pl.BlockSpec((rows, 1), lambda k, b: (0, 0)),
                pl.BlockSpec((tk, 2 * width), lambda k, b: (k, 0)),
                pl.BlockSpec((rows, width), lambda k, b: (0, 0)),
            ],
            out_specs=pl.BlockSpec((rows, width), lambda k, b: (0, 0)),
        ),
        input_output_aliases={4: 0},
        compiler_params=pltpu.CompilerParams(
            dimension_semantics=("arbitrary",), vmem_limit_bytes=60 * 1024 * 1024
        ),
        cost_estimate=pl.CostEstimate(
            flops=flops,
            transcendentals=rows * kv_rows * HEADS,
            bytes_accessed=kv_rows * 2 * width * 2 + rows * width * 10,
        ),
    )(base, queries, limits, kv, acc)


ORDER = (None, (0,1,0),(1,0,0),(1,1,0),(3,0,0),(3,1,0),(2,0,0),(2,1,0),(0,1,1),(1,0,1),(1,1,1),(3,0,1),(3,1,1),(2,0,1),(2,1,1),(0,0,1))


def fused_kernel(peers, key_rows, q_ref, lim_ref, gain_ref, cola_ref, colb_ref, hist_hbm, start_hbm,
                 x_hbm, gate_hbm, wout_hbm, out_ref, kv_buf, kv_sem, acc, normed, ret, part, xv, gv, wv,
                 send_sem, recv_sem, local_sem, start_sem, misc_sem):
    me = lax.axis_index("cand")
    uid = lax.axis_index("user")
    rows, width = q_ref.shape
    half_rows = rows // 2
    blk = half_rows // peers
    cap = 2 * blk
    head_size = width // HEADS
    half_scale = 0.5 / math.sqrt(head_size)
    segments = hist_hbm.shape[0] // key_rows - 1
    steps = 2 * segments
    own = lax.axis_index("user")

    barrier = pltpu.get_barrier_semaphore()
    for j in range(1, peers):
        pl.semaphore_signal(
            barrier, inc=1, device_id=(uid, lax.rem(me + j, peers)), device_id_type=pl.DeviceIdType.MESH
        )

    def start_copy(half):
        return pltpu.make_async_copy(
            start_hbm.at[pl.ds(half * half_rows, half_rows)], acc.at[half], start_sem.at[half]
        )

    def kv_copy(s, slot):
        k = lax.rem(own + 1 + lax.rem(s, segments), segments + 1)
        return pltpu.make_async_copy(
            hist_hbm.at[pl.ds(pl.multiple_of(k * key_rows, key_rows), key_rows)],
            kv_buf.at[slot],
            kv_sem.at[slot],
        )

    def peer(j, sign):
        dx, dy, dc = ORDER[j]
        core = lax.rem(me, 2)
        y_lo = lax.rem(me // 2, 2)
        x = me // 4
        return (
            lax.rem(x + sign * dx + 4, 4) * 4
            + lax.rem(y_lo + sign * dy + 2, 2) * 2
            + lax.rem(core + sign * dc + 2, 2)
        )

    def remote(half, j):
        p = peer(j, 1)
        return pltpu.make_async_remote_copy(
            src_ref=normed.at[half, pl.ds(pl.multiple_of(p * blk, blk), blk)],
            dst_ref=ret.at[half, pl.ds(pl.multiple_of(me * blk, blk), blk)],
            send_sem=send_sem.at[half, j],
            recv_sem=recv_sem.at[half, j],
            device_id=(uid, p),
            device_id_type=pl.DeviceIdType.MESH,
        )

    def incoming(half, j):
        src = peer(j, -1)
        return pltpu.make_async_remote_copy(
            src_ref=normed.at[half, pl.ds(pl.multiple_of(me * blk, blk), blk)],
            dst_ref=ret.at[half, pl.ds(pl.multiple_of(src * blk, blk), blk)],
            send_sem=send_sem.at[half, j],
            recv_sem=recv_sem.at[half, j],
            device_id=(uid, src),
            device_id_type=pl.DeviceIdType.MESH,
        )

    def local(half):
        return pltpu.make_async_copy(
            normed.at[half, pl.ds(pl.multiple_of(me * blk, blk), blk)],
            ret.at[half, pl.ds(pl.multiple_of(me * blk, blk), blk)],
            local_sem.at[half],
        )

    kv_copy(0, 0).start()
    start_copy(0).start()
    start_copy(1).start()
    misc = [
        pltpu.make_async_copy(src, dst, misc_sem.at[n])
        for n, (src, dst) in enumerate(((x_hbm, xv), (gate_hbm, gv), (wout_hbm, wv)))
    ]
    for copy in misc:
        copy.start()

    def tail(half, col_ref):
        homes = col_ref.shape[0]
        pick = lax.broadcasted_iota(jnp.int32, (homes, half_rows), 1) == col_ref[...]
        home = jnp.dot(pick.astype(jnp.bfloat16), ret[half], preferred_element_type=jnp.float32)
        mixed = (home * gv[...].astype(jnp.float32)).astype(jnp.bfloat16)
        return jnp.dot(mixed, wv[...], preferred_element_type=jnp.float32)

    for half in range(2):
        start_copy(half).wait()
        total = acc.at[half]

        def step(i, carry, half=half, total=total):
            s = half * segments + i
            slot = lax.rem(s, 2)
            k = lax.rem(own + 1 + i, segments + 1)
            kv_copy(s, slot).wait()

            @pl.when(s + 1 < steps)
            def _():
                kv_copy(s + 1, 1 - slot).start()

            q_rows = pl.ds(half * half_rows, half_rows)
            pos = k * key_rows + lax.broadcasted_iota(jnp.int32, (half_rows, key_rows), 1)
            vis = pos < lim_ref[q_rows, :]
            block = kv_buf.at[slot]
            for h in range(HEADS):
                cols = slice(h * head_size, (h + 1) * head_size)
                scores = lax.dot_general(
                    q_ref[q_rows, cols],
                    block[:, cols],
                    (((1,), (1,)), ((), ())),
                    preferred_element_type=jnp.float32,
                )
                t = scores * half_scale
                w = jnp.where(vis, t + t * jnp.tanh(t), 0.0).astype(jnp.bfloat16)
                vh = block[:, width + h * head_size : width + (h + 1) * head_size]
                total[:, cols] += jnp.dot(w, vh, preferred_element_type=jnp.float32)
            return carry

        lax.fori_loop(0, segments, step, 0)
        value = total[...]
        mean_row = jnp.mean(value, axis=1, keepdims=True)
        centered = value - mean_row
        variance = jnp.mean(centered * centered, axis=1, keepdims=True)
        scale_row = lax.rsqrt(variance + norm_eps)
        normed[half] = (centered * scale_row * gain_ref[...]).astype(jnp.bfloat16)
        if half == 0:
            pl.semaphore_wait(barrier, peers - 1)
        local(half).start()
        for j in range(1, peers):
            remote(half, j).start()


    for copy in misc:
        copy.wait()
    local(0).wait()
    for j in range(1, peers):
        incoming(0, j).wait_recv()
    part[...] = tail(0, cola_ref)
    local(1).wait()
    for j in range(1, peers):
        incoming(1, j).wait_recv()
    for half in range(2):
        for j in range(1, peers):
            remote(half, j).wait_send()
    out_ref[...] = (xv[...].astype(jnp.float32) + part[...] + tail(1, colb_ref)).astype(out_ref.dtype)


def attend_and_return(queries, limits, history, start, gain, cols, cand_x, gate, w_out, peers, key_rows):
    rows, width = queries.shape
    homes = cand_x.shape[0]
    kernel = functools.partial(fused_kernel, peers, key_rows)
    vmem = pl.BlockSpec(memory_space=pltpu.VMEM)
    hbm = pl.BlockSpec(memory_space=pl.ANY)
    return pl.pallas_call(
        kernel,
        out_shape=jax.ShapeDtypeStruct((homes, width), jnp.bfloat16),
        in_specs=[vmem, vmem, vmem, vmem, vmem, hbm, hbm, hbm, hbm, hbm],
        out_specs=vmem,
        scratch_shapes=[
            pltpu.VMEM((2, key_rows, 2 * width), jnp.bfloat16),
            pltpu.SemaphoreType.DMA((2,)),
            pltpu.VMEM((2, rows // 2, width), jnp.float32),
            pltpu.VMEM((2, rows // 2, width), jnp.bfloat16),
            pltpu.VMEM((2, rows // 2, width), jnp.bfloat16),
            pltpu.VMEM((homes, width), jnp.float32),
            pltpu.VMEM((homes, width), jnp.bfloat16),
            pltpu.VMEM((homes, width), jnp.bfloat16),
            pltpu.VMEM(w_out.shape, jnp.bfloat16),
            pltpu.SemaphoreType.DMA((2, peers)),
            pltpu.SemaphoreType.DMA((2, peers)),
            pltpu.SemaphoreType.DMA((2,)),
            pltpu.SemaphoreType.DMA((2,)),
            pltpu.SemaphoreType.DMA((3,)),
        ],
        compiler_params=pltpu.CompilerParams(
            collective_id=0, has_side_effects=True, vmem_limit_bytes=60 * 1024 * 1024
        ),
        cost_estimate=pl.CostEstimate(
            flops=8 * rows * history.shape[0] * width + 4 * homes * width * (rows + width),
            transcendentals=rows * history.shape[0] * HEADS,
            bytes_accessed=2 * history.size * 2 + rows * width * 6,
        ),
    )(queries, limits, gain.reshape(1, width), cols[0], cols[1], history, start, cand_x, gate, w_out)


def per_device(cand_x, cand_user, visible, hist_len, kv_cache, w_in, w_out, ln_gain):
    rows, width = cand_x.shape
    columns = lax.axis_size("cand")
    capacity = 2 * rows // columns
    slots = columns * capacity
    hidden = jax.nn.silu(jnp.dot(cand_x, w_in, preferred_element_type=jnp.float32))
    queries = hidden[:, :width].astype(jnp.bfloat16)
    gate = hidden[:, width:].astype(jnp.bfloat16)
    owner = cand_user[:, 0]
    onehot = (owner[:, None] == jnp.arange(columns, dtype=jnp.int32)[None, :]).astype(jnp.int32)
    earlier = jnp.cumsum(onehot, axis=0) - onehot
    slot_of = owner * capacity + jnp.sum(earlier * onehot, axis=1)
    send_rows = jnp.zeros((slots, width), jnp.bfloat16).at[slot_of].set(queries)
    send_vis = jnp.zeros((slots,), jnp.bfloat16).at[slot_of].set(visible.astype(jnp.bfloat16))
    got_rows, got_vis = (
        lax.all_to_all(
            send_rows.reshape(columns, capacity, width),
            "cand",
            split_axis=0,
            concat_axis=0,
            tiled=True,
        ),
        lax.all_to_all(
            send_vis.reshape(columns, capacity), "cand", split_axis=0, concat_axis=0, tiled=True
        ),
    )
    got_rows = got_rows.reshape(slots, width)
    got_vis = got_vis.reshape(slots)
    user_length = hist_len[0].astype(jnp.float32)
    limits = jnp.minimum(user_length, BLK * got_vis.astype(jnp.float32)).astype(jnp.int32)
    halves = lambda x: jnp.swapaxes(x.reshape(columns, 2, capacity // 2, -1), 0, 1).reshape(slots, -1)
    segment = kv_cache[0]
    me = lax.axis_index("user").astype(jnp.int32).reshape(1)
    queries_h = halves(got_rows)
    limits_h = halves(limits.reshape(slots, 1))
    start = attend(
        queries_h, limits_h, segment, jnp.zeros((slots, width), jnp.float32), me, segment.shape[0], False
    )
    history = lax.all_gather(segment, "user", axis=0, tiled=True)
    rank = slot_of - owner * capacity
    half_cap = capacity // 2
    cols = (
        jnp.where(rank < half_cap, owner * half_cap + rank, -1).reshape(rows, 1),
        jnp.where(rank >= half_cap, owner * half_cap + rank - half_cap, -1).reshape(rows, 1),
    )
    return attend_and_return(
        queries_h, limits_h, history, start, ln_gain, cols, cand_x, gate, w_out, columns, segment.shape[0]
    )


def solution(mesh):
    in_specs = (
        P(("user", "cand"), None),
        P(("user", "cand"), None),
        P(("user", "cand")),
        P("cand"),
        P("cand", "user", None),
        P(),
        P(),
        P(),
    )
    out_specs = P(("user", "cand"), None)
    return jax.shard_map(
        per_device, mesh=mesh, in_specs=in_specs, out_specs=out_specs, check_vma=False
    )
```

```python
import functools
import math

import jax
import jax.numpy as jnp
from jax import lax
from jax.experimental import pallas as pl
from jax.experimental.pallas import tpu as pltpu
from jax.sharding import PartitionSpec as P

HEADS = 8
BLK = 128
SUB_ROWS = 1024

norm_eps = 1e-06


def attend_kernel(seg_rows, skip_own, base_ref, q_ref, lim_ref, kv_ref, acc_ref, o_ref):
    k = pl.program_id(0)
    me = base_ref[0]
    width = q_ref.shape[1]
    head_size = width // HEADS
    tk = kv_ref.shape[0]
    rows = q_ref.shape[0]
    half_scale = 0.5 / math.sqrt(head_size)

    @pl.when(k == 0)
    def _():
        o_ref[...] = acc_ref[...]

    if skip_own:
        start = k * seg_rows
        run = k != me
    else:
        start = me * seg_rows + k * tk
        run = k >= 0

    @pl.when(run)
    def _():
        def sub(r, carry):
            r0 = pl.multiple_of(r * SUB_ROWS, SUB_ROWS)
            lim = lim_ref[pl.ds(r0, SUB_ROWS), :]
            pos = start + lax.broadcasted_iota(jnp.int32, (SUB_ROWS, tk), 1)
            vis = pos < lim
            for h in range(HEADS):
                cols = slice(h * head_size, (h + 1) * head_size)
                qh = q_ref[pl.ds(r0, SUB_ROWS), cols]
                kh = kv_ref[:, cols]
                s = lax.dot_general(
                    qh, kh, (((1,), (1,)), ((), ())), preferred_element_type=jnp.float32
                )
                t = s * half_scale
                w = jnp.where(vis, t + t * jnp.tanh(t), 0.0).astype(jnp.bfloat16)
                vh = kv_ref[:, width + h * head_size : width + (h + 1) * head_size]
                o_ref[pl.ds(r0, SUB_ROWS), cols] += jnp.dot(
                    w, vh, preferred_element_type=jnp.float32
                )
            return carry

        lax.fori_loop(0, rows // SUB_ROWS, sub, 0)


def attend(queries, limits, kv, acc, base, seg_rows, skip_own):
    rows, width = queries.shape
    kv_rows = kv.shape[0]
    tk = seg_rows
    steps = kv_rows // tk
    kernel = functools.partial(attend_kernel, seg_rows, skip_own)
    flops = 4 * rows * kv_rows * width
    return pl.pallas_call(
        kernel,
        out_shape=jax.ShapeDtypeStruct((rows, width), jnp.float32),
        grid_spec=pltpu.PrefetchScalarGridSpec(
            num_scalar_prefetch=1,
            grid=(steps,),
            in_specs=[
                pl.BlockSpec((rows, width), lambda k, b: (0, 0)),
                pl.BlockSpec((rows, 1), lambda k, b: (0, 0)),
                pl.BlockSpec((tk, 2 * width), lambda k, b: (k, 0)),
                pl.BlockSpec((rows, width), lambda k, b: (0, 0)),
            ],
            out_specs=pl.BlockSpec((rows, width), lambda k, b: (0, 0)),
        ),
        input_output_aliases={4: 0},
        compiler_params=pltpu.CompilerParams(
            dimension_semantics=("arbitrary",), vmem_limit_bytes=60 * 1024 * 1024
        ),
        cost_estimate=pl.CostEstimate(
            flops=flops,
            transcendentals=rows * kv_rows * HEADS,
            bytes_accessed=kv_rows * 2 * width * 2 + rows * width * 10,
        ),
    )(base, queries, limits, kv, acc)


ORDER = (None, (0,1,0),(1,0,0),(1,1,0),(3,0,0),(3,1,0),(2,0,0),(2,1,0),(0,1,1),(1,0,1),(1,1,1),(3,0,1),(3,1,1),(2,0,1),(2,1,1),(0,0,1))


def fused_kernel(peers, key_rows, q_ref, lim_ref, gain_ref, cola_ref, colb_ref, hist_hbm, start_hbm,
                 gate_hbm, wout_hbm, out_ref, kv_buf, kv_sem, acc, normed, ret, part, gv, wv,
                 send_sem, recv_sem, local_sem, start_sem, misc_sem):
    me = lax.axis_index("cand")
    uid = lax.axis_index("user")
    rows, width = q_ref.shape
    half_rows = rows // 2
    blk = half_rows // peers
    cap = 2 * blk
    head_size = width // HEADS
    half_scale = 0.5 / math.sqrt(head_size)
    segments = hist_hbm.shape[0] // key_rows - 1
    steps = 2 * segments
    own = lax.axis_index("user")

    barrier = pltpu.get_barrier_semaphore()
    for j in range(1, peers):
        pl.semaphore_signal(
            barrier, inc=1, device_id=(uid, lax.rem(me + j, peers)), device_id_type=pl.DeviceIdType.MESH
        )

    def start_copy(half):
        return pltpu.make_async_copy(
            start_hbm.at[pl.ds(half * half_rows, half_rows)], acc.at[half], start_sem.at[half]
        )

    def kv_copy(s, slot):
        k = lax.rem(own + 1 + lax.rem(s, segments), segments + 1)
        return pltpu.make_async_copy(
            hist_hbm.at[pl.ds(pl.multiple_of(k * key_rows, key_rows), key_rows)],
            kv_buf.at[slot],
            kv_sem.at[slot],
        )

    def peer(j, sign):
        dx, dy, dc = ORDER[j]
        core = lax.rem(me, 2)
        y_lo = lax.rem(me // 2, 2)
        x = me // 4
        return (
            lax.rem(x + sign * dx + 4, 4) * 4
            + lax.rem(y_lo + sign * dy + 2, 2) * 2
            + lax.rem(core + sign * dc + 2, 2)
        )

    def remote(half, j):
        p = peer(j, 1)
        return pltpu.make_async_remote_copy(
            src_ref=normed.at[half, pl.ds(pl.multiple_of(p * blk, blk), blk)],
            dst_ref=ret.at[half, pl.ds(pl.multiple_of(me * blk, blk), blk)],
            send_sem=send_sem.at[half, j],
            recv_sem=recv_sem.at[half, j],
            device_id=(uid, p),
            device_id_type=pl.DeviceIdType.MESH,
        )

    def incoming(half, j):
        src = peer(j, -1)
        return pltpu.make_async_remote_copy(
            src_ref=normed.at[half, pl.ds(pl.multiple_of(me * blk, blk), blk)],
            dst_ref=ret.at[half, pl.ds(pl.multiple_of(src * blk, blk), blk)],
            send_sem=send_sem.at[half, j],
            recv_sem=recv_sem.at[half, j],
            device_id=(uid, src),
            device_id_type=pl.DeviceIdType.MESH,
        )

    def local(half):
        return pltpu.make_async_copy(
            normed.at[half, pl.ds(pl.multiple_of(me * blk, blk), blk)],
            ret.at[half, pl.ds(pl.multiple_of(me * blk, blk), blk)],
            local_sem.at[half],
        )

    kv_copy(0, 0).start()
    start_copy(0).start()
    start_copy(1).start()
    misc = [
        pltpu.make_async_copy(src, dst, misc_sem.at[n])
        for n, (src, dst) in enumerate(((gate_hbm, gv), (wout_hbm, wv)))
    ]
    for copy in misc:
        copy.start()

    def tail(half, col_ref):
        homes = col_ref.shape[0]
        pick = lax.broadcasted_iota(jnp.int32, (homes, half_rows), 1) == col_ref[...]
        home = jnp.dot(pick.astype(jnp.bfloat16), ret[half], preferred_element_type=jnp.float32)
        mixed = (home * gv[...].astype(jnp.float32)).astype(jnp.bfloat16)
        return jnp.dot(mixed, wv[...], preferred_element_type=jnp.float32)

    for half in range(2):
        start_copy(half).wait()
        total = acc.at[half]

        def step(i, carry, half=half, total=total):
            s = half * segments + i
            slot = lax.rem(s, 2)
            k = lax.rem(own + 1 + i, segments + 1)
            kv_copy(s, slot).wait()

            @pl.when(s + 1 < steps)
            def _():
                kv_copy(s + 1, 1 - slot).start()

            q_rows = pl.ds(half * half_rows, half_rows)
            pos = k * key_rows + lax.broadcasted_iota(jnp.int32, (half_rows, key_rows), 1)
            vis = pos < lim_ref[q_rows, :]
            block = kv_buf.at[slot]
            for h in range(HEADS):
                cols = slice(h * head_size, (h + 1) * head_size)
                scores = lax.dot_general(
                    q_ref[q_rows, cols],
                    block[:, cols],
                    (((1,), (1,)), ((), ())),
                    preferred_element_type=jnp.float32,
                )
                t = scores * half_scale
                w = jnp.where(vis, t + t * jnp.tanh(t), 0.0).astype(jnp.bfloat16)
                vh = block[:, width + h * head_size : width + (h + 1) * head_size]
                total[:, cols] += jnp.dot(w, vh, preferred_element_type=jnp.float32)
            return carry

        lax.fori_loop(0, segments, step, 0)
        value = total[...]
        mean_row = jnp.mean(value, axis=1, keepdims=True)
        centered = value - mean_row
        variance = jnp.mean(centered * centered, axis=1, keepdims=True)
        scale_row = lax.rsqrt(variance + norm_eps)
        normed[half] = (centered * scale_row * gain_ref[...]).astype(jnp.bfloat16)
        if half == 0:
            pl.semaphore_wait(barrier, peers - 1)
        local(half).start()
        for j in range(1, peers):
            remote(half, j).start()


    for copy in misc:
        copy.wait()
    local(0).wait()
    for j in range(1, peers):
        incoming(0, j).wait_recv()
    part[...] = tail(0, cola_ref)
    local(1).wait()
    for j in range(1, peers):
        incoming(1, j).wait_recv()
    for half in range(2):
        for j in range(1, peers):
            remote(half, j).wait_send()
    out_ref[...] = part[...] + tail(1, colb_ref)


def attend_and_return(queries, limits, history, start, gain, cols, cand_x, gate, w_out, peers, key_rows):
    rows, width = queries.shape
    homes = cand_x.shape[0]
    kernel = functools.partial(fused_kernel, peers, key_rows)
    vmem = pl.BlockSpec(memory_space=pltpu.VMEM)
    hbm = pl.BlockSpec(memory_space=pl.ANY)
    return pl.pallas_call(
        kernel,
        out_shape=jax.ShapeDtypeStruct((homes, width), jnp.float32),
        in_specs=[vmem, vmem, vmem, vmem, vmem, hbm, hbm, hbm, hbm],
        out_specs=vmem,
        scratch_shapes=[
            pltpu.VMEM((2, key_rows, 2 * width), jnp.bfloat16),
            pltpu.SemaphoreType.DMA((2,)),
            pltpu.VMEM((2, rows // 2, width), jnp.float32),
            pltpu.VMEM((2, rows // 2, width), jnp.bfloat16),
            pltpu.VMEM((2, rows // 2, width), jnp.bfloat16),
            pltpu.VMEM((homes, width), jnp.float32),
            pltpu.VMEM((homes, width), jnp.bfloat16),
            pltpu.VMEM(w_out.shape, jnp.bfloat16),
            pltpu.SemaphoreType.DMA((2, peers)),
            pltpu.SemaphoreType.DMA((2, peers)),
            pltpu.SemaphoreType.DMA((2,)),
            pltpu.SemaphoreType.DMA((2,)),
            pltpu.SemaphoreType.DMA((2,)),
        ],
        compiler_params=pltpu.CompilerParams(
            collective_id=0, has_side_effects=True, vmem_limit_bytes=60 * 1024 * 1024
        ),
        cost_estimate=pl.CostEstimate(
            flops=8 * rows * history.shape[0] * width + 4 * homes * width * (rows + width),
            transcendentals=rows * history.shape[0] * HEADS,
            bytes_accessed=2 * history.size * 2 + rows * width * 6,
        ),
    )(queries, limits, gain.reshape(1, width), cols[0], cols[1], history, start, gate, w_out)


def per_device(cand_x, cand_user, visible, hist_len, kv_cache, w_in, w_out, ln_gain):
    rows, width = cand_x.shape
    columns = lax.axis_size("cand")
    capacity = 2 * rows // columns
    slots = columns * capacity
    hidden = jax.nn.silu(jnp.dot(cand_x, w_in, preferred_element_type=jnp.float32))
    queries = hidden[:, :width].astype(jnp.bfloat16)
    gate = hidden[:, width:].astype(jnp.bfloat16)
    owner = cand_user[:, 0]
    onehot = (owner[:, None] == jnp.arange(columns, dtype=jnp.int32)[None, :]).astype(jnp.int32)
    earlier = jnp.cumsum(onehot, axis=0) - onehot
    slot_of = owner * capacity + jnp.sum(earlier * onehot, axis=1)
    send_rows = jnp.zeros((slots, width), jnp.bfloat16).at[slot_of].set(queries)
    send_vis = jnp.zeros((slots,), jnp.bfloat16).at[slot_of].set(visible.astype(jnp.bfloat16))
    got_rows, got_vis = (
        lax.all_to_all(
            send_rows.reshape(columns, capacity, width),
            "cand",
            split_axis=0,
            concat_axis=0,
            tiled=True,
        ),
        lax.all_to_all(
            send_vis.reshape(columns, capacity), "cand", split_axis=0, concat_axis=0, tiled=True
        ),
    )
    got_rows = got_rows.reshape(slots, width)
    got_vis = got_vis.reshape(slots)
    user_length = hist_len[0].astype(jnp.float32)
    limits = jnp.minimum(user_length, BLK * got_vis.astype(jnp.float32)).astype(jnp.int32)
    halves = lambda x: jnp.swapaxes(x.reshape(columns, 2, capacity // 2, -1), 0, 1).reshape(slots, -1)
    segment = kv_cache[0]
    me = lax.axis_index("user").astype(jnp.int32).reshape(1)
    queries_h = halves(got_rows)
    limits_h = halves(limits.reshape(slots, 1))
    start = attend(
        queries_h, limits_h, segment, jnp.zeros((slots, width), jnp.float32), me, segment.shape[0], False
    )
    history = lax.all_gather(segment, "user", axis=0, tiled=True)
    rank = slot_of - owner * capacity
    half_cap = capacity // 2
    cols = (
        jnp.where(rank < half_cap, owner * half_cap + rank, -1).reshape(rows, 1),
        jnp.where(rank >= half_cap, owner * half_cap + rank - half_cap, -1).reshape(rows, 1),
    )
    projected = attend_and_return(
        queries_h, limits_h, history, start, ln_gain, cols, cand_x, gate, w_out, columns, segment.shape[0]
    )
    return (cand_x.astype(jnp.float32) + projected).astype(jnp.bfloat16)


def solution(mesh):
    in_specs = (
        P(("user", "cand"), None),
        P(("user", "cand"), None),
        P(("user", "cand")),
        P("cand"),
        P("cand", "user", None),
        P(),
        P(),
        P(),
    )
    out_specs = P(("user", "cand"), None)
    return jax.shard_map(
        per_device, mesh=mesh, in_specs=in_specs, out_specs=out_specs, check_vma=False
    )
```

```python
import functools
import math

import jax
import jax.numpy as jnp
from jax import lax
from jax.experimental import pallas as pl
from jax.experimental.pallas import tpu as pltpu
from jax.sharding import PartitionSpec as P

HEADS = 8
BLK = 128
SUB_ROWS = 1024

norm_eps = 1e-06


def attend_kernel(seg_rows, skip_own, base_ref, q_ref, lim_ref, kv_ref, acc_ref, o_ref):
    k = pl.program_id(0)
    me = base_ref[0]
    width = q_ref.shape[1]
    head_size = width // HEADS
    tk = kv_ref.shape[0]
    rows = q_ref.shape[0]
    half_scale = 0.5 / math.sqrt(head_size)

    @pl.when(k == 0)
    def _():
        o_ref[...] = acc_ref[...]

    if skip_own:
        start = k * seg_rows
        run = k != me
    else:
        start = me * seg_rows + k * tk
        run = k >= 0

    @pl.when(run)
    def _():
        def sub(r, carry):
            r0 = pl.multiple_of(r * SUB_ROWS, SUB_ROWS)
            lim = lim_ref[pl.ds(r0, SUB_ROWS), :]
            pos = start + lax.broadcasted_iota(jnp.int32, (SUB_ROWS, tk), 1)
            vis = pos < lim
            for h in range(HEADS):
                cols = slice(h * head_size, (h + 1) * head_size)
                qh = q_ref[pl.ds(r0, SUB_ROWS), cols]
                kh = kv_ref[:, cols]
                s = lax.dot_general(
                    qh, kh, (((1,), (1,)), ((), ())), preferred_element_type=jnp.float32
                )
                t = s * half_scale
                w = jnp.where(vis, t + t * jnp.tanh(t), 0.0).astype(jnp.bfloat16)
                vh = kv_ref[:, width + h * head_size : width + (h + 1) * head_size]
                o_ref[pl.ds(r0, SUB_ROWS), cols] += jnp.dot(
                    w, vh, preferred_element_type=jnp.float32
                )
            return carry

        lax.fori_loop(0, rows // SUB_ROWS, sub, 0)


def attend(queries, limits, kv, acc, base, seg_rows, skip_own):
    rows, width = queries.shape
    kv_rows = kv.shape[0]
    tk = seg_rows
    steps = kv_rows // tk
    kernel = functools.partial(attend_kernel, seg_rows, skip_own)
    flops = 4 * rows * kv_rows * width
    return pl.pallas_call(
        kernel,
        out_shape=jax.ShapeDtypeStruct((rows, width), jnp.float32),
        grid_spec=pltpu.PrefetchScalarGridSpec(
            num_scalar_prefetch=1,
            grid=(steps,),
            in_specs=[
                pl.BlockSpec((rows, width), lambda k, b: (0, 0)),
                pl.BlockSpec((rows, 1), lambda k, b: (0, 0)),
                pl.BlockSpec((tk, 2 * width), lambda k, b: (k, 0)),
                pl.BlockSpec((rows, width), lambda k, b: (0, 0)),
            ],
            out_specs=pl.BlockSpec((rows, width), lambda k, b: (0, 0)),
        ),
        input_output_aliases={4: 0},
        compiler_params=pltpu.CompilerParams(
            dimension_semantics=("arbitrary",), vmem_limit_bytes=60 * 1024 * 1024
        ),
        cost_estimate=pl.CostEstimate(
            flops=flops,
            transcendentals=rows * kv_rows * HEADS,
            bytes_accessed=kv_rows * 2 * width * 2 + rows * width * 10,
        ),
    )(base, queries, limits, kv, acc)


ORDER = (None, (0,1,0),(1,0,0),(1,1,0),(3,0,0),(3,1,0),(2,0,0),(2,1,0),(0,1,1),(1,0,1),(1,1,1),(3,0,1),(3,1,1),(2,0,1),(2,1,1),(0,0,1))


def fused_kernel(peers, key_rows, q_ref, lim_ref, gain_ref, cola_ref, colb_ref, hist_hbm, start_hbm,
                 x_hbm, gate_hbm, wout_hbm, out_ref, kv_buf, kv_sem, acc, normed, ret, part, xv, gv, wv,
                 send_sem, recv_sem, local_sem, start_sem, misc_sem):
    me = lax.axis_index("cand")
    uid = lax.axis_index("user")
    rows, width = q_ref.shape
    half_rows = rows // 2
    blk = half_rows // peers
    cap = 2 * blk
    head_size = width // HEADS
    half_scale = 0.5 / math.sqrt(head_size)
    segments = hist_hbm.shape[0] // key_rows - 1
    steps = 2 * segments
    own = lax.axis_index("user")

    barrier = pltpu.get_barrier_semaphore()
    for j in range(1, peers):
        pl.semaphore_signal(
            barrier, inc=1, device_id=(uid, lax.rem(me + j, peers)), device_id_type=pl.DeviceIdType.MESH
        )

    def start_copy(half):
        return pltpu.make_async_copy(
            start_hbm.at[pl.ds(half * half_rows, half_rows)], acc.at[half], start_sem.at[half]
        )

    def kv_copy(s, slot):
        k = lax.rem(own + 1 + lax.rem(s, segments), segments + 1)
        return pltpu.make_async_copy(
            hist_hbm.at[pl.ds(pl.multiple_of(k * key_rows, key_rows), key_rows)],
            kv_buf.at[slot],
            kv_sem.at[slot],
        )

    def peer(j, sign):
        dx, dy, dc = ORDER[j]
        core = lax.rem(me, 2)
        y_lo = lax.rem(me // 2, 2)
        x = me // 4
        return (
            lax.rem(x + sign * dx + 4, 4) * 4
            + lax.rem(y_lo + sign * dy + 2, 2) * 2
            + lax.rem(core + sign * dc + 2, 2)
        )

    def remote(half, j):
        p = peer(j, 1)
        return pltpu.make_async_remote_copy(
            src_ref=normed.at[half, pl.ds(pl.multiple_of(p * blk, blk), blk)],
            dst_ref=ret.at[half, pl.ds(pl.multiple_of(me * blk, blk), blk)],
            send_sem=send_sem.at[half, j],
            recv_sem=recv_sem.at[half, j],
            device_id=(uid, p),
            device_id_type=pl.DeviceIdType.MESH,
        )

    def incoming(half, j):
        src = peer(j, -1)
        return pltpu.make_async_remote_copy(
            src_ref=normed.at[half, pl.ds(pl.multiple_of(me * blk, blk), blk)],
            dst_ref=ret.at[half, pl.ds(pl.multiple_of(src * blk, blk), blk)],
            send_sem=send_sem.at[half, j],
            recv_sem=recv_sem.at[half, j],
            device_id=(uid, src),
            device_id_type=pl.DeviceIdType.MESH,
        )

    def local(half):
        return pltpu.make_async_copy(
            normed.at[half, pl.ds(pl.multiple_of(me * blk, blk), blk)],
            ret.at[half, pl.ds(pl.multiple_of(me * blk, blk), blk)],
            local_sem.at[half],
        )

    kv_copy(0, 0).start()
    start_copy(0).start()
    start_copy(1).start()
    misc = [
        pltpu.make_async_copy(src, dst, misc_sem.at[n])
        for n, (src, dst) in enumerate(((x_hbm, xv), (gate_hbm, gv), (wout_hbm, wv)))
    ]
    for copy in misc:
        copy.start()

    def tail(half, col_ref):
        homes = col_ref.shape[0]
        pick = lax.broadcasted_iota(jnp.int32, (homes, half_rows), 1) == col_ref[...]
        home = jnp.dot(pick.astype(jnp.bfloat16), ret[half], preferred_element_type=jnp.float32)
        mixed = (home * gv[...].astype(jnp.float32)).astype(jnp.bfloat16)
        return jnp.dot(mixed, wv[...], preferred_element_type=jnp.float32)

    for half in range(2):
        start_copy(half).wait()
        total = acc.at[half]

        def step(i, carry, half=half, total=total):
            s = half * segments + i
            slot = lax.rem(s, 2)
            k = lax.rem(own + 1 + i, segments + 1)
            kv_copy(s, slot).wait()

            @pl.when(s + 1 < steps)
            def _():
                kv_copy(s + 1, 1 - slot).start()

            q_rows = pl.ds(half * half_rows, half_rows)
            pos = k * key_rows + lax.broadcasted_iota(jnp.int32, (half_rows, key_rows), 1)
            vis = pos < lim_ref[q_rows, :]
            block = kv_buf.at[slot]
            for h in range(HEADS):
                cols = slice(h * head_size, (h + 1) * head_size)
                scores = lax.dot_general(
                    q_ref[q_rows, cols],
                    block[:, cols],
                    (((1,), (1,)), ((), ())),
                    preferred_element_type=jnp.float32,
                )
                t = scores * half_scale
                w = jnp.where(vis, t + t * jnp.tanh(t), 0.0).astype(jnp.bfloat16)
                vh = block[:, width + h * head_size : width + (h + 1) * head_size]
                total[:, cols] += jnp.dot(w, vh, preferred_element_type=jnp.float32)
            return carry

        lax.fori_loop(0, segments, step, 0)
        value = total[...]
        mean_row = jnp.mean(value, axis=1, keepdims=True)
        centered = value - mean_row
        variance = jnp.mean(centered * centered, axis=1, keepdims=True)
        scale_row = lax.rsqrt(variance + norm_eps)
        normed[half] = (centered * scale_row * gain_ref[...]).astype(jnp.bfloat16)
        if half == 0:
            pl.semaphore_wait(barrier, peers - 1)
        local(half).start()
        for j in range(1, peers):
            remote(half, j).start()


    for copy in misc:
        copy.wait()
    local(0).wait()
    for j in range(1, peers):
        incoming(0, j).wait_recv()
    part[...] = tail(0, cola_ref)
    local(1).wait()
    for j in range(1, peers):
        incoming(1, j).wait_recv()
    out_ref[...] = (xv[...].astype(jnp.float32) + part[...] + tail(1, colb_ref)).astype(out_ref.dtype)
    for half in range(2):
        for j in range(1, peers):
            remote(half, j).wait_send()


def attend_and_return(queries, limits, history, start, gain, cols, cand_x, gate, w_out, peers, key_rows):
    rows, width = queries.shape
    homes = cand_x.shape[0]
    kernel = functools.partial(fused_kernel, peers, key_rows)
    vmem = pl.BlockSpec(memory_space=pltpu.VMEM)
    hbm = pl.BlockSpec(memory_space=pl.ANY)
    return pl.pallas_call(
        kernel,
        out_shape=jax.ShapeDtypeStruct((homes, width), jnp.bfloat16),
        in_specs=[vmem, vmem, vmem, vmem, vmem, hbm, hbm, hbm, hbm, hbm],
        out_specs=vmem,
        scratch_shapes=[
            pltpu.VMEM((2, key_rows, 2 * width), jnp.bfloat16),
            pltpu.SemaphoreType.DMA((2,)),
            pltpu.VMEM((2, rows // 2, width), jnp.float32),
            pltpu.VMEM((2, rows // 2, width), jnp.bfloat16),
            pltpu.VMEM((2, rows // 2, width), jnp.bfloat16),
            pltpu.VMEM((homes, width), jnp.float32),
            pltpu.VMEM((homes, width), jnp.bfloat16),
            pltpu.VMEM((homes, width), jnp.bfloat16),
            pltpu.VMEM(w_out.shape, jnp.bfloat16),
            pltpu.SemaphoreType.DMA((2, peers)),
            pltpu.SemaphoreType.DMA((2, peers)),
            pltpu.SemaphoreType.DMA((2,)),
            pltpu.SemaphoreType.DMA((2,)),
            pltpu.SemaphoreType.DMA((3,)),
        ],
        compiler_params=pltpu.CompilerParams(
            collective_id=0, has_side_effects=True, vmem_limit_bytes=60 * 1024 * 1024
        ),
        cost_estimate=pl.CostEstimate(
            flops=8 * rows * history.shape[0] * width + 4 * homes * width * (rows + width),
            transcendentals=rows * history.shape[0] * HEADS,
            bytes_accessed=2 * history.size * 2 + rows * width * 6,
        ),
    )(queries, limits, gain.reshape(1, width), cols[0], cols[1], history, start, cand_x, gate, w_out)


def per_device(cand_x, cand_user, visible, hist_len, kv_cache, w_in, w_out, ln_gain):
    rows, width = cand_x.shape
    columns = lax.axis_size("cand")
    capacity = 2 * rows // columns
    slots = columns * capacity
    hidden = jax.nn.silu(jnp.dot(cand_x, w_in, preferred_element_type=jnp.float32))
    queries = hidden[:, :width].astype(jnp.bfloat16)
    gate = hidden[:, width:].astype(jnp.bfloat16)
    owner = cand_user[:, 0]
    onehot = (owner[:, None] == jnp.arange(columns, dtype=jnp.int32)[None, :]).astype(jnp.int32)
    earlier = jnp.cumsum(onehot, axis=0) - onehot
    slot_of = owner * capacity + jnp.sum(earlier * onehot, axis=1)
    send_rows = jnp.zeros((slots, width), jnp.bfloat16).at[slot_of].set(queries)
    send_vis = jnp.zeros((slots,), jnp.bfloat16).at[slot_of].set(visible.astype(jnp.bfloat16))
    got_rows, got_vis = (
        lax.all_to_all(
            send_rows.reshape(columns, capacity, width),
            "cand",
            split_axis=0,
            concat_axis=0,
            tiled=True,
        ),
        lax.all_to_all(
            send_vis.reshape(columns, capacity), "cand", split_axis=0, concat_axis=0, tiled=True
        ),
    )
    got_rows = got_rows.reshape(slots, width)
    got_vis = got_vis.reshape(slots)
    user_length = hist_len[0].astype(jnp.float32)
    limits = jnp.minimum(user_length, BLK * got_vis.astype(jnp.float32)).astype(jnp.int32)
    halves = lambda x: jnp.swapaxes(x.reshape(columns, 2, capacity // 2, -1), 0, 1).reshape(slots, -1)
    segment = kv_cache[0]
    me = lax.axis_index("user").astype(jnp.int32).reshape(1)
    queries_h = halves(got_rows)
    limits_h = halves(limits.reshape(slots, 1))
    start = attend(
        queries_h, limits_h, segment, jnp.zeros((slots, width), jnp.float32), me, segment.shape[0], False
    )
    history = lax.all_gather(segment, "user", axis=0, tiled=True)
    rank = slot_of - owner * capacity
    half_cap = capacity // 2
    cols = (
        jnp.where(rank < half_cap, owner * half_cap + rank, -1).reshape(rows, 1),
        jnp.where(rank >= half_cap, owner * half_cap + rank - half_cap, -1).reshape(rows, 1),
    )
    return attend_and_return(
        queries_h, limits_h, history, start, ln_gain, cols, cand_x, gate, w_out, columns, segment.shape[0]
    )


def solution(mesh):
    in_specs = (
        P(("user", "cand"), None),
        P(("user", "cand"), None),
        P(("user", "cand")),
        P("cand"),
        P("cand", "user", None),
        P(),
        P(),
        P(),
    )
    out_specs = P(("user", "cand"), None)
    return jax.shard_map(
        per_device, mesh=mesh, in_specs=in_specs, out_specs=out_specs, check_vma=False
    )
```

```python
import functools
import math

import jax
import jax.numpy as jnp
from jax import lax
from jax.experimental import pallas as pl
from jax.experimental.pallas import tpu as pltpu
from jax.sharding import PartitionSpec as P

HEADS = 8
BLK = 128
SUB_ROWS = 1024

norm_eps = 1e-06


def attend_kernel(seg_rows, skip_own, base_ref, q_ref, lim_ref, kv_ref, acc_ref, o_ref):
    k = pl.program_id(0)
    me = base_ref[0]
    width = q_ref.shape[1]
    head_size = width // HEADS
    tk = kv_ref.shape[0]
    rows = q_ref.shape[0]
    half_scale = 0.5 / math.sqrt(head_size)

    @pl.when(k == 0)
    def _():
        o_ref[...] = acc_ref[...]

    if skip_own:
        start = k * seg_rows
        run = k != me
    else:
        start = me * seg_rows + k * tk
        run = k >= 0

    @pl.when(run)
    def _():
        def sub(r, carry):
            r0 = pl.multiple_of(r * SUB_ROWS, SUB_ROWS)
            lim = lim_ref[pl.ds(r0, SUB_ROWS), :]
            pos = start + lax.broadcasted_iota(jnp.int32, (SUB_ROWS, tk), 1)
            vis = pos < lim
            for h in range(HEADS):
                cols = slice(h * head_size, (h + 1) * head_size)
                qh = q_ref[pl.ds(r0, SUB_ROWS), cols]
                kh = kv_ref[:, cols]
                s = lax.dot_general(
                    qh, kh, (((1,), (1,)), ((), ())), preferred_element_type=jnp.float32
                )
                t = s * half_scale
                w = jnp.where(vis, t + t * jnp.tanh(t), 0.0).astype(jnp.bfloat16)
                vh = kv_ref[:, width + h * head_size : width + (h + 1) * head_size]
                o_ref[pl.ds(r0, SUB_ROWS), cols] += jnp.dot(
                    w, vh, preferred_element_type=jnp.float32
                )
            return carry

        lax.fori_loop(0, rows // SUB_ROWS, sub, 0)


def attend(queries, limits, kv, acc, base, seg_rows, skip_own):
    rows, width = queries.shape
    kv_rows = kv.shape[0]
    tk = seg_rows
    steps = kv_rows // tk
    kernel = functools.partial(attend_kernel, seg_rows, skip_own)
    flops = 4 * rows * kv_rows * width
    return pl.pallas_call(
        kernel,
        out_shape=jax.ShapeDtypeStruct((rows, width), jnp.float32),
        grid_spec=pltpu.PrefetchScalarGridSpec(
            num_scalar_prefetch=1,
            grid=(steps,),
            in_specs=[
                pl.BlockSpec((rows, width), lambda k, b: (0, 0)),
                pl.BlockSpec((rows, 1), lambda k, b: (0, 0)),
                pl.BlockSpec((tk, 2 * width), lambda k, b: (k, 0)),
                pl.BlockSpec((rows, width), lambda k, b: (0, 0)),
            ],
            out_specs=pl.BlockSpec((rows, width), lambda k, b: (0, 0)),
        ),
        input_output_aliases={4: 0},
        compiler_params=pltpu.CompilerParams(
            dimension_semantics=("arbitrary",), vmem_limit_bytes=60 * 1024 * 1024
        ),
        cost_estimate=pl.CostEstimate(
            flops=flops,
            transcendentals=rows * kv_rows * HEADS,
            bytes_accessed=kv_rows * 2 * width * 2 + rows * width * 10,
        ),
    )(base, queries, limits, kv, acc)


ORDER = (None, (0,1,0),(1,0,0),(1,1,0),(3,0,0),(3,1,0),(2,0,0),(2,1,0),(0,1,1),(1,0,1),(1,1,1),(3,0,1),(3,1,1),(2,0,1),(2,1,1),(0,0,1))


def fused_kernel(peers, key_rows, q_ref, lim_ref, gain_ref, cola_ref, colb_ref, hist_hbm, start_hbm,
                 x_hbm, gate_hbm, wout_hbm, out_ref, kv_buf, kv_sem, acc, normed, ret, part, xv, gv, wv,
                 send_sem, recv_sem, local_sem, start_sem, misc_sem):
    me = lax.axis_index("cand")
    uid = lax.axis_index("user")
    rows, width = q_ref.shape
    half_rows = rows // 2
    blk = half_rows // peers
    cap = 2 * blk
    head_size = width // HEADS
    half_scale = 0.5 / math.sqrt(head_size)
    segments = hist_hbm.shape[0] // key_rows - 1
    steps = 2 * segments
    own = lax.axis_index("user")

    barrier = pltpu.get_barrier_semaphore()
    for j in range(1, peers):
        pl.semaphore_signal(
            barrier, inc=1, device_id=(uid, lax.rem(me + j, peers)), device_id_type=pl.DeviceIdType.MESH
        )

    def start_copy(half):
        return pltpu.make_async_copy(
            start_hbm.at[pl.ds(half * half_rows, half_rows)], acc.at[half], start_sem.at[half]
        )

    def kv_copy(s, slot):
        k = lax.rem(own + 1 + lax.rem(s, segments), segments + 1)
        return pltpu.make_async_copy(
            hist_hbm.at[pl.ds(pl.multiple_of(k * key_rows, key_rows), key_rows)],
            kv_buf.at[slot],
            kv_sem.at[slot],
        )

    def peer(j, sign):
        dx, dy, dc = ORDER[j]
        core = lax.rem(me, 2)
        y_lo = lax.rem(me // 2, 2)
        x = me // 4
        return (
            lax.rem(x + sign * dx + 4, 4) * 4
            + lax.rem(y_lo + sign * dy + 2, 2) * 2
            + lax.rem(core + sign * dc + 2, 2)
        )

    def remote(half, j):
        p = peer(j, 1)
        return pltpu.make_async_remote_copy(
            src_ref=normed.at[half, pl.ds(pl.multiple_of(p * blk, blk), blk)],
            dst_ref=ret.at[half, pl.ds(pl.multiple_of(me * blk, blk), blk)],
            send_sem=send_sem.at[half, j],
            recv_sem=recv_sem.at[half, j],
            device_id=(uid, p),
            device_id_type=pl.DeviceIdType.MESH,
        )

    def incoming(half, j):
        src = peer(j, -1)
        return pltpu.make_async_remote_copy(
            src_ref=normed.at[half, pl.ds(pl.multiple_of(me * blk, blk), blk)],
            dst_ref=ret.at[half, pl.ds(pl.multiple_of(src * blk, blk), blk)],
            send_sem=send_sem.at[half, j],
            recv_sem=recv_sem.at[half, j],
            device_id=(uid, src),
            device_id_type=pl.DeviceIdType.MESH,
        )

    def local(half):
        return pltpu.make_async_copy(
            normed.at[half, pl.ds(pl.multiple_of(me * blk, blk), blk)],
            ret.at[half, pl.ds(pl.multiple_of(me * blk, blk), blk)],
            local_sem.at[half],
        )

    kv_copy(0, 0).start()
    start_copy(0).start()
    start_copy(1).start()
    misc = [
        pltpu.make_async_copy(src, dst, misc_sem.at[n])
        for n, (src, dst) in enumerate(((x_hbm, xv), (gate_hbm, gv), (wout_hbm, wv)))
    ]

    def tail(half, col_ref):
        homes = col_ref.shape[0]
        pick = lax.broadcasted_iota(jnp.int32, (homes, half_rows), 1) == col_ref[...]
        home = jnp.dot(pick.astype(jnp.bfloat16), ret[half], preferred_element_type=jnp.float32)
        mixed = (home * gv[...].astype(jnp.float32)).astype(jnp.bfloat16)
        return jnp.dot(mixed, wv[...], preferred_element_type=jnp.float32)

    for half in range(2):
        start_copy(half).wait()
        total = acc.at[half]

        def step(i, carry, half=half, total=total):
            s = half * segments + i
            slot = lax.rem(s, 2)
            k = lax.rem(own + 1 + i, segments + 1)
            kv_copy(s, slot).wait()

            @pl.when(s + 1 < steps)
            def _():
                kv_copy(s + 1, 1 - slot).start()

            q_rows = pl.ds(half * half_rows, half_rows)
            pos = k * key_rows + lax.broadcasted_iota(jnp.int32, (half_rows, key_rows), 1)
            vis = pos < lim_ref[q_rows, :]
            block = kv_buf.at[slot]
            for h in range(HEADS):
                cols = slice(h * head_size, (h + 1) * head_size)
                scores = lax.dot_general(
                    q_ref[q_rows, cols],
                    block[:, cols],
                    (((1,), (1,)), ((), ())),
                    preferred_element_type=jnp.float32,
                )
                t = scores * half_scale
                w = jnp.where(vis, t + t * jnp.tanh(t), 0.0).astype(jnp.bfloat16)
                vh = block[:, width + h * head_size : width + (h + 1) * head_size]
                total[:, cols] += jnp.dot(w, vh, preferred_element_type=jnp.float32)
            return carry

        lax.fori_loop(0, segments, step, 0)
        if half == 0:
            for copy in misc:
                copy.start()
        value = total[...]
        mean_row = jnp.mean(value, axis=1, keepdims=True)
        centered = value - mean_row
        variance = jnp.mean(centered * centered, axis=1, keepdims=True)
        scale_row = lax.rsqrt(variance + norm_eps)
        normed[half] = (centered * scale_row * gain_ref[...]).astype(jnp.bfloat16)
        if half == 0:
            pl.semaphore_wait(barrier, peers - 1)
        local(half).start()
        for j in range(1, peers):
            remote(half, j).start()


    for copy in misc:
        copy.wait()
    local(0).wait()
    for j in range(1, peers):
        incoming(0, j).wait_recv()
    part[...] = tail(0, cola_ref)
    local(1).wait()
    for j in range(1, peers):
        incoming(1, j).wait_recv()
    for half in range(2):
        for j in range(1, peers):
            remote(half, j).wait_send()
    out_ref[...] = (xv[...].astype(jnp.float32) + part[...] + tail(1, colb_ref)).astype(out_ref.dtype)


def attend_and_return(queries, limits, history, start, gain, cols, cand_x, gate, w_out, peers, key_rows):
    rows, width = queries.shape
    homes = cand_x.shape[0]
    kernel = functools.partial(fused_kernel, peers, key_rows)
    vmem = pl.BlockSpec(memory_space=pltpu.VMEM)
    hbm = pl.BlockSpec(memory_space=pl.ANY)
    return pl.pallas_call(
        kernel,
        out_shape=jax.ShapeDtypeStruct((homes, width), jnp.bfloat16),
        in_specs=[vmem, vmem, vmem, vmem, vmem, hbm, hbm, hbm, hbm, hbm],
        out_specs=vmem,
        scratch_shapes=[
            pltpu.VMEM((2, key_rows, 2 * width), jnp.bfloat16),
            pltpu.SemaphoreType.DMA((2,)),
            pltpu.VMEM((2, rows // 2, width), jnp.float32),
            pltpu.VMEM((2, rows // 2, width), jnp.bfloat16),
            pltpu.VMEM((2, rows // 2, width), jnp.bfloat16),
            pltpu.VMEM((homes, width), jnp.float32),
            pltpu.VMEM((homes, width), jnp.bfloat16),
            pltpu.VMEM((homes, width), jnp.bfloat16),
            pltpu.VMEM(w_out.shape, jnp.bfloat16),
            pltpu.SemaphoreType.DMA((2, peers)),
            pltpu.SemaphoreType.DMA((2, peers)),
            pltpu.SemaphoreType.DMA((2,)),
            pltpu.SemaphoreType.DMA((2,)),
            pltpu.SemaphoreType.DMA((3,)),
        ],
        compiler_params=pltpu.CompilerParams(
            collective_id=0, has_side_effects=True, vmem_limit_bytes=60 * 1024 * 1024
        ),
        cost_estimate=pl.CostEstimate(
            flops=8 * rows * history.shape[0] * width + 4 * homes * width * (rows + width),
            transcendentals=rows * history.shape[0] * HEADS,
            bytes_accessed=2 * history.size * 2 + rows * width * 6,
        ),
    )(queries, limits, gain.reshape(1, width), cols[0], cols[1], history, start, cand_x, gate, w_out)


def per_device(cand_x, cand_user, visible, hist_len, kv_cache, w_in, w_out, ln_gain):
    rows, width = cand_x.shape
    columns = lax.axis_size("cand")
    capacity = 2 * rows // columns
    slots = columns * capacity
    hidden = jax.nn.silu(jnp.dot(cand_x, w_in, preferred_element_type=jnp.float32))
    queries = hidden[:, :width].astype(jnp.bfloat16)
    gate = hidden[:, width:].astype(jnp.bfloat16)
    owner = cand_user[:, 0]
    onehot = (owner[:, None] == jnp.arange(columns, dtype=jnp.int32)[None, :]).astype(jnp.int32)
    earlier = jnp.cumsum(onehot, axis=0) - onehot
    slot_of = owner * capacity + jnp.sum(earlier * onehot, axis=1)
    send_rows = jnp.zeros((slots, width), jnp.bfloat16).at[slot_of].set(queries)
    send_vis = jnp.zeros((slots,), jnp.bfloat16).at[slot_of].set(visible.astype(jnp.bfloat16))
    got_rows, got_vis = (
        lax.all_to_all(
            send_rows.reshape(columns, capacity, width),
            "cand",
            split_axis=0,
            concat_axis=0,
            tiled=True,
        ),
        lax.all_to_all(
            send_vis.reshape(columns, capacity), "cand", split_axis=0, concat_axis=0, tiled=True
        ),
    )
    got_rows = got_rows.reshape(slots, width)
    got_vis = got_vis.reshape(slots)
    user_length = hist_len[0].astype(jnp.float32)
    limits = jnp.minimum(user_length, BLK * got_vis.astype(jnp.float32)).astype(jnp.int32)
    halves = lambda x: jnp.swapaxes(x.reshape(columns, 2, capacity // 2, -1), 0, 1).reshape(slots, -1)
    segment = kv_cache[0]
    me = lax.axis_index("user").astype(jnp.int32).reshape(1)
    queries_h = halves(got_rows)
    limits_h = halves(limits.reshape(slots, 1))
    start = attend(
        queries_h, limits_h, segment, jnp.zeros((slots, width), jnp.float32), me, segment.shape[0], False
    )
    history = lax.all_gather(segment, "user", axis=0, tiled=True)
    rank = slot_of - owner * capacity
    half_cap = capacity // 2
    cols = (
        jnp.where(rank < half_cap, owner * half_cap + rank, -1).reshape(rows, 1),
        jnp.where(rank >= half_cap, owner * half_cap + rank - half_cap, -1).reshape(rows, 1),
    )
    return attend_and_return(
        queries_h, limits_h, history, start, ln_gain, cols, cand_x, gate, w_out, columns, segment.shape[0]
    )


def solution(mesh):
    in_specs = (
        P(("user", "cand"), None),
        P(("user", "cand"), None),
        P(("user", "cand")),
        P("cand"),
        P("cand", "user", None),
        P(),
        P(),
        P(),
    )
    out_specs = P(("user", "cand"), None)
    return jax.shard_map(
        per_device, mesh=mesh, in_specs=in_specs, out_specs=out_specs, check_vma=False
    )
```

```python
import functools
import math

import jax
import jax.numpy as jnp
from jax import lax
from jax.experimental import pallas as pl
from jax.experimental.pallas import tpu as pltpu
from jax.sharding import PartitionSpec as P

HEADS = 8
BLK = 128
SUB_ROWS = 1024

norm_eps = 1e-06


def attend_kernel(seg_rows, skip_own, base_ref, q_ref, lim_ref, kv_ref, acc_ref, o_ref):
    k = pl.program_id(0)
    me = base_ref[0]
    width = q_ref.shape[1]
    head_size = width // HEADS
    tk = kv_ref.shape[0]
    rows = q_ref.shape[0]
    half_scale = 0.5 / math.sqrt(head_size)

    @pl.when(k == 0)
    def _():
        o_ref[...] = acc_ref[...]

    if skip_own:
        start = k * seg_rows
        run = k != me
    else:
        start = me * seg_rows + k * tk
        run = k >= 0

    @pl.when(run)
    def _():
        def sub(r, carry):
            r0 = pl.multiple_of(r * SUB_ROWS, SUB_ROWS)
            lim = lim_ref[pl.ds(r0, SUB_ROWS), :]
            pos = start + lax.broadcasted_iota(jnp.int32, (SUB_ROWS, tk), 1)
            vis = pos < lim
            for h in range(HEADS):
                cols = slice(h * head_size, (h + 1) * head_size)
                qh = q_ref[pl.ds(r0, SUB_ROWS), cols]
                kh = kv_ref[:, cols]
                s = lax.dot_general(
                    qh, kh, (((1,), (1,)), ((), ())), preferred_element_type=jnp.float32
                )
                t = s * half_scale
                w = jnp.where(vis, t + t * jnp.tanh(t), 0.0).astype(jnp.bfloat16)
                vh = kv_ref[:, width + h * head_size : width + (h + 1) * head_size]
                o_ref[pl.ds(r0, SUB_ROWS), cols] += jnp.dot(
                    w, vh, preferred_element_type=jnp.float32
                )
            return carry

        lax.fori_loop(0, rows // SUB_ROWS, sub, 0)


def attend(queries, limits, kv, acc, base, seg_rows, skip_own):
    rows, width = queries.shape
    kv_rows = kv.shape[0]
    tk = seg_rows
    steps = kv_rows // tk
    kernel = functools.partial(attend_kernel, seg_rows, skip_own)
    flops = 4 * rows * kv_rows * width
    return pl.pallas_call(
        kernel,
        out_shape=jax.ShapeDtypeStruct((rows, width), jnp.float32),
        grid_spec=pltpu.PrefetchScalarGridSpec(
            num_scalar_prefetch=1,
            grid=(steps,),
            in_specs=[
                pl.BlockSpec((rows, width), lambda k, b: (0, 0)),
                pl.BlockSpec((rows, 1), lambda k, b: (0, 0)),
                pl.BlockSpec((tk, 2 * width), lambda k, b: (k, 0)),
                pl.BlockSpec((rows, width), lambda k, b: (0, 0)),
            ],
            out_specs=pl.BlockSpec((rows, width), lambda k, b: (0, 0)),
        ),
        input_output_aliases={4: 0},
        compiler_params=pltpu.CompilerParams(
            dimension_semantics=("arbitrary",), vmem_limit_bytes=60 * 1024 * 1024
        ),
        cost_estimate=pl.CostEstimate(
            flops=flops,
            transcendentals=rows * kv_rows * HEADS,
            bytes_accessed=kv_rows * 2 * width * 2 + rows * width * 10,
        ),
    )(base, queries, limits, kv, acc)


ORDER = (None, (0,1,0),(1,0,0),(1,1,0),(3,0,0),(3,1,0),(2,0,0),(2,1,0),(0,1,1),(1,0,1),(1,1,1),(3,0,1),(3,1,1),(2,0,1),(2,1,1),(0,0,1))


def fused_kernel(peers, key_rows, q_ref, lim_ref, gain_ref, cola_ref, colb_ref, hist_hbm, start_hbm,
                 x_hbm, gate_hbm, wout_hbm, out_ref, kv_buf, kv_sem, acc, normed, ret, part, xv, gv, wv,
                 sbuf, send_sem, recv_sem, local_sem, start_sem, misc_sem):
    me = lax.axis_index("cand")
    uid = lax.axis_index("user")
    rows, width = q_ref.shape
    half_rows = rows // 2
    blk = half_rows // peers
    cap = 2 * blk
    head_size = width // HEADS
    half_scale = 0.5 / math.sqrt(head_size)
    segments = hist_hbm.shape[0] // key_rows - 1
    steps = 2 * segments
    own = lax.axis_index("user")

    barrier = pltpu.get_barrier_semaphore()
    for j in range(1, peers):
        pl.semaphore_signal(
            barrier, inc=1, device_id=(uid, lax.rem(me + j, peers)), device_id_type=pl.DeviceIdType.MESH
        )

    def start_copy(half):
        return pltpu.make_async_copy(
            start_hbm.at[pl.ds(half * half_rows, half_rows)],
            sbuf if half == 0 else acc.at[half],
            start_sem.at[half],
        )

    def kv_copy(s, slot):
        k = lax.rem(own + 1 + lax.rem(s, segments), segments + 1)
        return pltpu.make_async_copy(
            hist_hbm.at[pl.ds(pl.multiple_of(k * key_rows, key_rows), key_rows)],
            kv_buf.at[slot],
            kv_sem.at[slot],
        )

    def peer(j, sign):
        dx, dy, dc = ORDER[j]
        core = lax.rem(me, 2)
        y_lo = lax.rem(me // 2, 2)
        x = me // 4
        return (
            lax.rem(x + sign * dx + 4, 4) * 4
            + lax.rem(y_lo + sign * dy + 2, 2) * 2
            + lax.rem(core + sign * dc + 2, 2)
        )

    def remote(half, j):
        p = peer(j, 1)
        return pltpu.make_async_remote_copy(
            src_ref=normed.at[half, pl.ds(pl.multiple_of(p * blk, blk), blk)],
            dst_ref=ret.at[half, pl.ds(pl.multiple_of(me * blk, blk), blk)],
            send_sem=send_sem.at[half, j],
            recv_sem=recv_sem.at[half, j],
            device_id=(uid, p),
            device_id_type=pl.DeviceIdType.MESH,
        )

    def incoming(half, j):
        src = peer(j, -1)
        return pltpu.make_async_remote_copy(
            src_ref=normed.at[half, pl.ds(pl.multiple_of(me * blk, blk), blk)],
            dst_ref=ret.at[half, pl.ds(pl.multiple_of(src * blk, blk), blk)],
            send_sem=send_sem.at[half, j],
            recv_sem=recv_sem.at[half, j],
            device_id=(uid, src),
            device_id_type=pl.DeviceIdType.MESH,
        )

    def local(half):
        return pltpu.make_async_copy(
            normed.at[half, pl.ds(pl.multiple_of(me * blk, blk), blk)],
            ret.at[half, pl.ds(pl.multiple_of(me * blk, blk), blk)],
            local_sem.at[half],
        )

    kv_copy(0, 0).start()
    start_copy(0).start()
    start_copy(1).start()
    misc = [
        pltpu.make_async_copy(src, dst, misc_sem.at[n])
        for n, (src, dst) in enumerate(((x_hbm, xv), (gate_hbm, gv), (wout_hbm, wv)))
    ]

    def tail(half, col_ref):
        homes = col_ref.shape[0]
        pick = lax.broadcasted_iota(jnp.int32, (homes, half_rows), 1) == col_ref[...]
        home = jnp.dot(pick.astype(jnp.bfloat16), ret[half], preferred_element_type=jnp.float32)
        mixed = (home * gv[...].astype(jnp.float32)).astype(jnp.bfloat16)
        return jnp.dot(mixed, wv[...], preferred_element_type=jnp.float32)

    for half in range(2):
        total = acc.at[half]
        if half == 0:
            total[...] = jnp.zeros_like(total)
        else:
            start_copy(half).wait()

        def step(i, carry, half=half, total=total):
            s = half * segments + i
            slot = lax.rem(s, 2)
            k = lax.rem(own + 1 + i, segments + 1)
            kv_copy(s, slot).wait()

            @pl.when(s + 1 < steps)
            def _():
                kv_copy(s + 1, 1 - slot).start()

            q_rows = pl.ds(half * half_rows, half_rows)
            pos = k * key_rows + lax.broadcasted_iota(jnp.int32, (half_rows, key_rows), 1)
            vis = pos < lim_ref[q_rows, :]
            block = kv_buf.at[slot]
            for h in range(HEADS):
                cols = slice(h * head_size, (h + 1) * head_size)
                scores = lax.dot_general(
                    q_ref[q_rows, cols],
                    block[:, cols],
                    (((1,), (1,)), ((), ())),
                    preferred_element_type=jnp.float32,
                )
                t = scores * half_scale
                w = jnp.where(vis, t + t * jnp.tanh(t), 0.0).astype(jnp.bfloat16)
                vh = block[:, width + h * head_size : width + (h + 1) * head_size]
                total[:, cols] += jnp.dot(w, vh, preferred_element_type=jnp.float32)
            return carry

        lax.fori_loop(0, segments, step, 0)
        if half == 0:
            for copy in misc:
                copy.start()
        if half == 0:
            start_copy(0).wait()
            value = total[...] + sbuf[...]
        else:
            value = total[...]
        mean_row = jnp.mean(value, axis=1, keepdims=True)
        centered = value - mean_row
        variance = jnp.mean(centered * centered, axis=1, keepdims=True)
        scale_row = lax.rsqrt(variance + norm_eps)
        normed[half] = (centered * scale_row * gain_ref[...]).astype(jnp.bfloat16)
        if half == 0:
            pl.semaphore_wait(barrier, peers - 1)
        local(half).start()
        for j in range(1, peers):
            remote(half, j).start()


    for copy in misc:
        copy.wait()
    local(0).wait()
    for j in range(1, peers):
        incoming(0, j).wait_recv()
    part[...] = tail(0, cola_ref)
    local(1).wait()
    for j in range(1, peers):
        incoming(1, j).wait_recv()
    for half in range(2):
        for j in range(1, peers):
            remote(half, j).wait_send()
    out_ref[...] = (xv[...].astype(jnp.float32) + part[...] + tail(1, colb_ref)).astype(out_ref.dtype)


def attend_and_return(queries, limits, history, start, gain, cols, cand_x, gate, w_out, peers, key_rows):
    rows, width = queries.shape
    homes = cand_x.shape[0]
    kernel = functools.partial(fused_kernel, peers, key_rows)
    vmem = pl.BlockSpec(memory_space=pltpu.VMEM)
    hbm = pl.BlockSpec(memory_space=pl.ANY)
    return pl.pallas_call(
        kernel,
        out_shape=jax.ShapeDtypeStruct((homes, width), jnp.bfloat16),
        in_specs=[vmem, vmem, vmem, vmem, vmem, hbm, hbm, hbm, hbm, hbm],
        out_specs=vmem,
        scratch_shapes=[
            pltpu.VMEM((2, key_rows, 2 * width), jnp.bfloat16),
            pltpu.SemaphoreType.DMA((2,)),
            pltpu.VMEM((2, rows // 2, width), jnp.float32),
            pltpu.VMEM((2, rows // 2, width), jnp.bfloat16),
            pltpu.VMEM((2, rows // 2, width), jnp.bfloat16),
            pltpu.VMEM((homes, width), jnp.float32),
            pltpu.VMEM((homes, width), jnp.bfloat16),
            pltpu.VMEM((homes, width), jnp.bfloat16),
            pltpu.VMEM(w_out.shape, jnp.bfloat16),
            pltpu.VMEM((rows // 2, width), jnp.float32),
            pltpu.SemaphoreType.DMA((2, peers)),
            pltpu.SemaphoreType.DMA((2, peers)),
            pltpu.SemaphoreType.DMA((2,)),
            pltpu.SemaphoreType.DMA((2,)),
            pltpu.SemaphoreType.DMA((3,)),
        ],
        compiler_params=pltpu.CompilerParams(
            collective_id=0, has_side_effects=True, vmem_limit_bytes=60 * 1024 * 1024
        ),
        cost_estimate=pl.CostEstimate(
            flops=8 * rows * history.shape[0] * width + 4 * homes * width * (rows + width),
            transcendentals=rows * history.shape[0] * HEADS,
            bytes_accessed=2 * history.size * 2 + rows * width * 6,
        ),
    )(queries, limits, gain.reshape(1, width), cols[0], cols[1], history, start, cand_x, gate, w_out)


def per_device(cand_x, cand_user, visible, hist_len, kv_cache, w_in, w_out, ln_gain):
    rows, width = cand_x.shape
    columns = lax.axis_size("cand")
    capacity = 2 * rows // columns
    slots = columns * capacity
    hidden = jax.nn.silu(jnp.dot(cand_x, w_in, preferred_element_type=jnp.float32))
    queries = hidden[:, :width].astype(jnp.bfloat16)
    gate = hidden[:, width:].astype(jnp.bfloat16)
    owner = cand_user[:, 0]
    onehot = (owner[:, None] == jnp.arange(columns, dtype=jnp.int32)[None, :]).astype(jnp.int32)
    earlier = jnp.cumsum(onehot, axis=0) - onehot
    slot_of = owner * capacity + jnp.sum(earlier * onehot, axis=1)
    send_rows = jnp.zeros((slots, width), jnp.bfloat16).at[slot_of].set(queries)
    send_vis = jnp.zeros((slots,), jnp.bfloat16).at[slot_of].set(visible.astype(jnp.bfloat16))
    got_rows, got_vis = (
        lax.all_to_all(
            send_rows.reshape(columns, capacity, width),
            "cand",
            split_axis=0,
            concat_axis=0,
            tiled=True,
        ),
        lax.all_to_all(
            send_vis.reshape(columns, capacity), "cand", split_axis=0, concat_axis=0, tiled=True
        ),
    )
    got_rows = got_rows.reshape(slots, width)
    got_vis = got_vis.reshape(slots)
    user_length = hist_len[0].astype(jnp.float32)
    limits = jnp.minimum(user_length, BLK * got_vis.astype(jnp.float32)).astype(jnp.int32)
    halves = lambda x: jnp.swapaxes(x.reshape(columns, 2, capacity // 2, -1), 0, 1).reshape(slots, -1)
    segment = kv_cache[0]
    me = lax.axis_index("user").astype(jnp.int32).reshape(1)
    queries_h = halves(got_rows)
    limits_h = halves(limits.reshape(slots, 1))
    start = attend(
        queries_h, limits_h, segment, jnp.zeros((slots, width), jnp.float32), me, segment.shape[0], False
    )
    history = lax.all_gather(segment, "user", axis=0, tiled=True)
    rank = slot_of - owner * capacity
    half_cap = capacity // 2
    cols = (
        jnp.where(rank < half_cap, owner * half_cap + rank, -1).reshape(rows, 1),
        jnp.where(rank >= half_cap, owner * half_cap + rank - half_cap, -1).reshape(rows, 1),
    )
    return attend_and_return(
        queries_h, limits_h, history, start, ln_gain, cols, cand_x, gate, w_out, columns, segment.shape[0]
    )


def solution(mesh):
    in_specs = (
        P(("user", "cand"), None),
        P(("user", "cand"), None),
        P(("user", "cand")),
        P("cand"),
        P("cand", "user", None),
        P(),
        P(),
        P(),
    )
    out_specs = P(("user", "cand"), None)
    return jax.shard_map(
        per_device, mesh=mesh, in_specs=in_specs, out_specs=out_specs, check_vma=False
    )
```
